128 devices in a mesh: group: 16 (over y, x), depth: 2 (over core), mp: 4 (over z).
Axes of the slice: x: 4, y: 4, z: 4, core: 2. Of those that a mesh axis runs over, the one named last changes fastest.
Arguments:
- states: bfloat16 [256, 4096], P(('group', 'depth', 'mp')), may hold values from -6 to 6
- queries: bfloat16 [256, 32, 128], P('group', 'mp'), may hold values from -6 to 6
- new_keys: bfloat16 [256, 8, 128], P('group', 'mp'), may hold values from -18 to 18
- new_values: bfloat16 [256, 8, 128], P('group', 'mp'), may hold values from -24 to 24
- text_keys: bfloat16 [256, 8, 512, 128], P('group', 'mp', 'depth'), may hold values from -6 to 6
- text_values: bfloat16 [256, 8, 512, 128], P('group', 'mp', 'depth'), may hold values from -24 to 24
- text_length: int32 [256], P('group'), may hold values from 2 to 512
- image_keys: bfloat16 [128, 8, 576, 128], P('group', 'mp'), may hold values from -6 to 6
- image_values: bfloat16 [128, 8, 576, 128], P('group', 'mp'), may hold values from -24 to 24
- image_slot: int32 [128], replicated, may hold values from 0 to 127, as said below
- block_list: int32 [16, 32], replicated, may hold values from 0 to 127, as said below
- block_count: int32 [16], replicated, may hold values from 16 to 32, as said below
- image_first: int32 [256], P('group'), may hold values from 0 to 31, as said below
- image_count: int32 [256], P('group'), may hold values from 1 to 2
- out_weight: bfloat16 [4096, 4096], P('mp'), may hold values from -0.09375 to 0.09375
- norm_gain: float32 [4096], replicated, may hold values from 0.5 to 1.5
- gate_weight: bfloat16 [4096, 14336], P(None, ('group', 'mp')), may hold values from -0.09375 to 0.09375
- up_weight: bfloat16 [4096, 14336], P(None, ('group', 'mp')), may hold values from -0.09375 to 0.09375
- down_weight: bfloat16 [14336, 4096], P(('group', 'mp')), may hold values from -0.046875 to 0.046875
Outputs:
- attention: bfloat16 [256, 32, 128], P(('group', 'depth'), 'mp')
- layer_out: bfloat16 [256, 4096], P(('group', 'depth', 'mp'))
The draws below stay inside these ranges and needn't reach their ends.
Inputs may be any that keep to these rules, and one draw needn't show every extreme that they name: `image_slot`: a permutation. The owner group of hash k is image_slot[k] // 8. `block_list`: the hashes of one group's list are distinct. Among one group's places with the same remainder modulo 2, at most 1 belongs to any one owner group; some group has block_count 32, and there every owner group holds exactly 1 place of every remainder. `block_count`: the sum of image_count over the group's requests. The requests of a group take consecutive list places in request order: image_first is the sum of image_count over the group's earlier requests.
All inputs are finite; a program needn't handle non-finite values.
Results may differ from the reference program's by a relative error of at most 0.012.
Values may be sent and summed in bfloat16 or wider, within the bound.
No kernel may reach another device: no remote copies, remote signals or barrier semaphores. Data moves between devices by JAX's collectives and lax.ppermute only.
A program may use at most 128 MiB of HBM per device.

```python
import math
import jax
import jax.numpy as jnp
from jax import lax

D = 4096
HQ = 32
KVH = 8
HD = 128
FF = 14336
PATCHES = 576
REQ = 16
IMG_DEV = 8
GROUPS = 16
DEPTHS = 2
BATCH = 256
LTEXT = 512
IMAGES = 128
LIST = 32
CAP = 1


def routing_plan(key):
    slot_order = jax.random.permutation(jax.random.fold_in(key, 101), IMAGES).astype(jnp.int32)
    hash_at = jnp.argsort(slot_order, stable=True).astype(jnp.int32)
    picked = jax.random.randint(jax.random.fold_in(key, 102), (GROUPS, REQ), 1, 3, dtype=jnp.int32)
    fullest = jax.random.randint(jax.random.fold_in(key, 103), (), 0, GROUPS, dtype=jnp.int32)
    picked = jnp.where(jnp.arange(GROUPS, dtype=jnp.int32)[:, None] == fullest, 2, picked).astype(jnp.int32)
    starts = (jnp.cumsum(picked, axis=1) - picked).astype(jnp.int32)
    totals = jnp.sum(picked, axis=1).astype(jnp.int32)
    order_keys = jax.random.split(jax.random.fold_in(key, 104), GROUPS * DEPTHS)
    orderings = jax.vmap(lambda single: jax.random.permutation(single, GROUPS * CAP))(order_keys)
    orderings = orderings.reshape(GROUPS, DEPTHS, GROUPS * CAP).astype(jnp.int32)
    owners = orderings % GROUPS
    copy_index = orderings // GROUPS
    pick_keys = jax.random.split(jax.random.fold_in(key, 105), GROUPS * GROUPS)
    inner_orders = jax.vmap(lambda single: jax.random.permutation(single, IMG_DEV))(pick_keys)
    inner_orders = inner_orders.reshape(GROUPS, GROUPS, IMG_DEV).astype(jnp.int32)
    column = jnp.arange(DEPTHS, dtype=jnp.int32)[None, :, None] * CAP + copy_index
    group_axis = jnp.arange(GROUPS, dtype=jnp.int32)[:, None, None]
    within = inner_orders[group_axis, owners, column]
    slot_rows = owners * IMG_DEV + within
    hashes = hash_at[slot_rows]
    listing = jnp.transpose(hashes, (0, 2, 1)).reshape(GROUPS, LIST).astype(jnp.int32)
    return (slot_order, listing, totals, starts.reshape(-1), picked.reshape(-1))


def draw_image_slot(key, part):
    return routing_plan(key)[0]


def draw_block_list(key, part):
    return routing_plan(key)[1]


def draw_block_count(key, part):
    return routing_plan(key)[2]


def draw_image_first(key, part):
    return routing_plan(key)[3]


def draw_image_count(key, part):
    return routing_plan(key)[4]


def draw_queries(key, part):
    values = jnp.clip(jax.random.normal(jax.random.fold_in(key, 203), (BATCH, HQ, HD), jnp.float32), -6.0, 6.0)
    return values.astype(jnp.bfloat16)


def draw_text_keys(key, part):
    values = jnp.clip(jax.random.normal(jax.random.fold_in(key, 205), (BATCH, KVH, LTEXT, HD), jnp.float32), -6.0, 6.0)
    return values.astype(jnp.bfloat16)


def with_ends(drawn, rng, low, largest):
    longest = drawn.shape.index(max(drawn.shape))
    spots = []
    for shift in (0, 1):
        where = [jax.random.randint(jax.random.fold_in(rng, axis), (), 0, length) for axis, length in enumerate(drawn.shape)]
        where[longest] = (where[longest] + shift) % drawn.shape[longest]
        spots.append(tuple(where))
    return drawn.at[spots[0]].set(low).at[spots[1]].set(largest)


def steps_of(stream_key, shape, shards, least, high):
    level, own = 1.0, jax.random.fold_in(stream_key, 6)
    for position, parts in shards:
        draws = jnp.exp(jax.random.uniform(jax.random.fold_in(own, position), (parts,), jnp.float32, least / len(shards), high / len(shards)))
        level = level * jnp.repeat(draws, shape[position] // parts).reshape([-1 if axis == position else 1 for axis in range(len(shape))])
    return level


def gaussian(rng, extent, scale, limit, cuts=(), kind=jnp.bfloat16):
    factor_of = steps_of(rng, extent, cuts, -0.22, 0.18) if cuts else 1.0
    array = jax.random.normal(rng, extent, jnp.float32) * scale * factor_of
    return jnp.minimum(jnp.maximum(array, -limit), limit).astype(kind)


def setup_inputs(seed: int = 0) -> dict:
    keys = jax.random.split(jax.random.key(seed), 20)
    states = gaussian(keys[0], (BATCH, D), 1.0, 6.0, ((0, 128),))
    queries = draw_queries(jax.random.fold_in(keys[19], 71), 0)
    new_keys = gaussian(keys[2], (BATCH, KVH, HD), 3.0, 18.0, ((0, 16), (1, 4)))
    new_values = gaussian(keys[3], (BATCH, KVH, HD), 4.0, 24.0, ((0, 16), (1, 4)))
    text_keys = draw_text_keys(jax.random.fold_in(keys[19], 71), 0)
    text_values = gaussian(keys[5], (BATCH, KVH, LTEXT, HD), 4.0, 24.0, ((0, 16), (1, 4), (2, 2)))
    text_length = with_ends(jax.random.randint(keys[6], (BATCH,), 2, LTEXT + 1), jax.random.fold_in(keys[6], 1), 2, LTEXT).astype(jnp.int32)
    image_keys = gaussian(keys[7], (IMAGES, KVH, PATCHES, HD), 1.0, 6.0, ((0, 16), (1, 4)))
    image_values = gaussian(keys[8], (IMAGES, KVH, PATCHES, HD), 4.0, 24.0, ((0, 16), (1, 4)))
    image_slot = draw_image_slot(jax.random.fold_in(keys[19], 71), 0)
    block_list = draw_block_list(jax.random.fold_in(keys[19], 71), 0)
    block_count = draw_block_count(jax.random.fold_in(keys[19], 71), 0)
    image_first = draw_image_first(jax.random.fold_in(keys[19], 71), 0)
    image_count = draw_image_count(jax.random.fold_in(keys[19], 71), 0)
    out_weight = gaussian(keys[14], (HQ * HD, D), (HQ * HD) ** -0.5, 0.09375, ((0, 4),))
    norm_gain = jnp.clip(1.0 + 0.1 * jax.random.normal(keys[15], (D,), jnp.float32), 0.5, 1.5)
    gate_weight = gaussian(keys[16], (D, FF), D ** -0.5, 0.09375, ((1, 64),))
    up_weight = gaussian(keys[17], (D, FF), D ** -0.5, 0.09375, ((1, 64),))
    down_weight = gaussian(keys[18], (FF, D), FF ** -0.5, 0.046875, ((0, 64),))
    return dict(states=states, queries=queries, new_keys=new_keys, new_values=new_values, text_keys=text_keys, text_values=text_values, text_length=text_length, image_keys=image_keys, image_values=image_values, image_slot=image_slot, block_list=block_list, block_count=block_count, image_first=image_first, image_count=image_count, out_weight=out_weight, norm_gain=norm_gain, gate_weight=gate_weight, up_weight=up_weight, down_weight=down_weight)


LOG_TWO = math.log(2.0)
MASKED_SCORE = -1e+30
NORM_EPSILON = 1e-05

def reference(states, queries, new_keys, new_values, text_keys, text_values, text_length, image_keys, image_values, image_slot, block_list, block_count, image_first, image_count, out_weight, norm_gain, gate_weight, up_weight, down_weight):
    share = HQ // KVH
    scaling = 1.0 / math.sqrt(HD)

    def one_group(group_index):
        offset = (group_index * REQ).astype(jnp.int32)
        grouped = lax.dynamic_slice_in_dim(queries, offset, REQ, 0).astype(jnp.float32).reshape(REQ, KVH, share, HD)
        text_key_rows = lax.dynamic_slice_in_dim(text_keys, offset, REQ, 0).astype(jnp.float32)
        text_value_rows = lax.dynamic_slice_in_dim(text_values, offset, REQ, 0).astype(jnp.float32)
        new_key_rows = lax.dynamic_slice_in_dim(new_keys, offset, REQ, 0).astype(jnp.float32)
        new_value_rows = lax.dynamic_slice_in_dim(new_values, offset, REQ, 0).astype(jnp.float32)
        lengths = lax.dynamic_slice_in_dim(text_length, offset, REQ, 0)
        starts = lax.dynamic_slice_in_dim(image_first, offset, REQ, 0)
        image_total = lax.dynamic_slice_in_dim(image_count, offset, REQ, 0)
        hashes = block_list[group_index]
        slot_rows = jnp.take(image_slot, hashes, axis=0)
        image_key_rows = jnp.take(image_keys, slot_rows, axis=0).astype(jnp.float32)
        image_value_rows = jnp.take(image_values, slot_rows, axis=0).astype(jnp.float32)
        text_scores = jnp.einsum('rhgd,rhpd->rhgp', grouped, text_key_rows) * scaling
        new_scores = jnp.einsum('rhgd,rhd->rhg', grouped, new_key_rows) * scaling
        image_scores = jnp.einsum('rhgd,jhpd->rhgjp', grouped, image_key_rows) * scaling
        image_scores = image_scores.reshape(REQ, KVH, share, LIST * PATCHES)
        scores = jnp.concatenate([text_scores, new_scores[..., None], image_scores], axis=-1)
        text_mask = jnp.arange(LTEXT, dtype=jnp.int32)[None, :] < lengths[:, None]
        positions = jnp.arange(LIST, dtype=jnp.int32)[None, :]
        image_mask = (positions >= starts[:, None]) & (positions < (starts + image_total)[:, None]) & (positions < block_count[group_index])
        image_mask = jnp.repeat(image_mask, PATCHES, axis=1)
        new_mask = jnp.ones((REQ, 1), dtype=bool)
        allowed = jnp.concatenate([text_mask, new_mask, image_mask], axis=1)[:, None, None, :]
        masked = jnp.where(allowed, scores, MASKED_SCORE)
        highest = lax.optimization_barrier(jnp.max(masked, axis=-1, keepdims=True))
        levels = jnp.floor(highest / LOG_TWO)
        weights = jnp.where(allowed, jnp.exp(scores - LOG_TWO * levels), 0.0).astype(jnp.bfloat16)
        weights = lax.optimization_barrier(weights).astype(jnp.float32)
        totals = lax.optimization_barrier(jnp.sum(weights, axis=-1))
        text_weights = weights[..., :LTEXT]
        new_weights = weights[..., LTEXT]
        image_weights = weights[..., LTEXT + 1:].reshape(REQ, KVH, share, LIST, PATCHES)
        summed = jnp.einsum('rhgp,rhpd->rhgd', text_weights, text_value_rows)
        summed = summed + new_weights[..., None] * new_value_rows[:, :, None, :]
        summed = summed + jnp.einsum('rhgjp,jhpd->rhgd', image_weights, image_value_rows)
        return (summed / totals[..., None]).reshape(REQ, HQ, HD).astype(jnp.bfloat16)
    attention = lax.map(one_group, jnp.arange(GROUPS, dtype=jnp.int32)).reshape(BATCH, HQ, HD)
    projected = jnp.dot(attention.reshape(BATCH, HQ * HD), out_weight, preferred_element_type=jnp.float32)
    residual = states.astype(jnp.float32) + projected
    spread = lax.optimization_barrier(jnp.mean(residual * residual, axis=-1, keepdims=True))
    normed = (residual * lax.rsqrt(spread + NORM_EPSILON) * norm_gain.astype(jnp.float32)).astype(jnp.bfloat16)
    gate_term = jnp.dot(normed, gate_weight, preferred_element_type=jnp.float32)
    up_term = jnp.dot(normed, up_weight, preferred_element_type=jnp.float32)
    hidden = (jax.nn.silu(gate_term) * up_term).astype(jnp.bfloat16)
    result = residual + jnp.dot(hidden, down_weight, preferred_element_type=jnp.float32)
    return (attention, result.astype(jnp.bfloat16))
```

```python
import functools
import math

import jax
import jax.numpy as jnp
from jax import lax
from jax.experimental import pallas as pl
from jax.experimental.pallas import tpu as pltpu
from jax.sharding import PartitionSpec as P

MASKED = -1e30
NORM_EPSILON = 1e-05
BF16 = jnp.bfloat16
F32 = jnp.float32
VMEM = pl.BlockSpec(memory_space=pltpu.VMEM)
SMEM = pl.BlockSpec(memory_space=pltpu.SMEM)


def call(kernel, out_shape, in_specs, flops, nbytes, name, scratch=(), vmem=16 << 20):
    return pl.pallas_call(
        kernel,
        out_shape=out_shape,
        in_specs=in_specs,
        out_specs=jax.tree.map(lambda _: VMEM, out_shape),
        scratch_shapes=list(scratch),
        cost_estimate=pl.CostEstimate(flops=flops, bytes_accessed=nbytes, transcendentals=0),
        compiler_params=pltpu.CompilerParams(vmem_limit_bytes=vmem),
        name=name,
    )


def matmul(a, b):
    return lax.dot_general(a, b, (((1,), (0,)), ((), ())), preferred_element_type=F32)


def matmul_t(a, b):
    return lax.dot_general(a, b, (((1,), (1,)), ((), ())), preferred_element_type=F32)


class Tables:
    def __init__(self, ref):
        self.ref = ref
        self.group, self.depth, self.mp = ref[0], ref[1], ref[2]

    def count(self):
        return self.ref[COUNT + self.group]

    def first(self, r):
        return self.ref[FIRST + r]

    def images(self, r):
        return self.ref[IMAGES + r]

    def length(self, r):
        return self.ref[LENGTH + r]

    def source(self, place):
        block = self.ref[BLOCKS + self.group * 32 + jnp.minimum(place, 31)]
        slot = self.ref[SLOTS + block]
        return slot >> 3, slot & 7


SLOTS, BLOCKS, COUNT, FIRST, IMAGES, LENGTH = 8, 136, 648, 664, 680, 696


def route_kernel(table, queries, out):
    t = Tables(table)
    count, depth = t.count(), t.depth
    requests = queries.shape[0]
    out[...] = jnp.full(out.shape, -1.0, BF16)
    for r in range(requests):
        start = t.first(r)
        skip = (start + depth) & 1
        place = start + skip
        owner, within = t.source(place)

        @pl.when((skip < t.images(r)) & (place < count))
        def _():
            out[owner, 0:8, :] = queries[r]
            code = (within * 2 + r // (requests // 2)).astype(F32)
            out[owner, 8:16, :] = jnp.full((8, 128), code, F32).astype(BF16)


def text_kernel(table, queries, new_keys, new_values, keys, values, own, other):
    t = Tables(table)
    depth = t.depth
    half = queries.shape[0] // 2
    heads, width = queries.shape[1:]
    span = keys.shape[2]
    scale = 1.0 / (math.sqrt(width) * math.log(2.0))
    for out, part in ((own, depth), (other, 1 - depth)):
        low = lax.broadcasted_iota(jnp.int32, (heads, 1), 0) < heads // 2
        scores, fresh = [], []
        for j in range(half):
            r = part * half + j
            q = queries[r]
            s = jnp.where(low, matmul_t(q, keys[r, 0]), matmul_t(q, keys[r, 1])) * scale
            at = depth * span + lax.broadcasted_iota(jnp.int32, (heads, span), 1)
            scores.append(jnp.where(at < t.length(r), s, MASKED))
            nk = new_keys[r].astype(F32)
            nk = jnp.where(low, nk[0:1], nk[1:2])
            fresh.append(jnp.sum(q.astype(F32) * nk, axis=-1, keepdims=True) * scale)
        s = jnp.concatenate(scores, axis=0)
        n = jnp.where(depth == 0, jnp.concatenate(fresh, axis=0), MASKED)
        level = jnp.floor(jnp.maximum(jnp.max(s, axis=-1, keepdims=True), n))
        w = jnp.where(s > 0.5 * MASKED, jnp.exp2(s - level), 0.0).astype(BF16)
        nw = jnp.where(n > 0.5 * MASKED, jnp.exp2(n - level), 0.0).astype(BF16).astype(F32)
        total = jnp.sum(w.astype(F32), axis=-1, keepdims=True) + nw
        lane = lax.broadcasted_iota(jnp.int32, (heads, 128), 1)
        for j in range(half):
            r = part * half + j
            rows = slice(j * heads, (j + 1) * heads)
            o = jnp.where(low, matmul(w[rows], values[r, 0]), matmul(w[rows], values[r, 1]))
            nv = new_values[r].astype(F32)
            o = o + nw[rows] * jnp.where(low, nv[0:1], nv[1:2])
            out[j, 0:8, :] = o
            out[j, 8:16, :] = jnp.where(lane < 64, level[rows], total[rows])


def image_kernel(arrived, keys, values, out):
    groups = arrived.shape[0]
    rows = groups * 8
    images, _, patches, width = keys.shape
    scale = 1.0 / (math.sqrt(width) * math.log(2.0))
    q = arrived[:, 0:8, :].reshape(rows, width)
    code = arrived[:, 8:16, :].reshape(rows, width).astype(F32)
    within = jnp.floor(code * 0.5)
    low = lax.broadcasted_iota(jnp.int32, (rows, 1), 0) % 8 < 4
    level = jnp.zeros((rows, 1), F32)
    total = jnp.zeros((rows, 1), F32)
    o = jnp.zeros((rows, width), F32)
    for i in range(images):
        mine = within[:, 0:1] == float(i)
        s = jnp.where(low, matmul_t(q, keys[i, 0]), matmul_t(q, keys[i, 1])) * scale
        here = jnp.floor(jnp.max(s, axis=-1, keepdims=True))
        w = jnp.where(mine, jnp.exp2(s - here), 0.0).astype(BF16)
        total = total + jnp.sum(w.astype(F32), axis=-1, keepdims=True)
        level = jnp.where(mine, here, level)
        o = o + jnp.where(low, matmul(w, values[i, 0]), matmul(w, values[i, 1]))
    o = o / jnp.where(total > 0.0, total, 1.0)
    lane = lax.broadcasted_iota(jnp.int32, (rows, width), 1)
    level_high = level.astype(BF16).astype(F32)
    total_high = total.astype(BF16).astype(F32)
    stats = jnp.where(
        lane < 64,
        jnp.where(lane < 32, level_high, level - level_high),
        jnp.where(lane < 96, total_high, total - total_high),
    )
    second = code - 2.0 * within
    o3 = o.astype(BF16).reshape(groups, 8, width)
    for h in range(2):
        out[:, h, 0:8, :] = o3
        out[:, h, 8:16, :] = (
            jnp.where(second == float(h), stats, 0.0).astype(BF16).reshape(groups, 8, width)
        )


def merge_kernel(table, back, own, other, out):
    t = Tables(table)
    count, depth = t.count(), t.depth
    half = own.shape[0]
    for j in range(half):
        r = depth * half + j
        parts = []
        for ref in (own, other):
            stats = ref[j, 8:16, :]
            parts.append((stats[:, 0:1], stats[:, 64:65], ref[j, 0:8, :]))
        for k in range(2):
            place = t.first(r) + k
            owner, _ = t.source(place)
            live = (k < t.images(r)) & (place < count)
            at = owner * 2 + (place & 1)
            stats = back[at, 8:16, :].astype(F32)
            level = jnp.where(live, stats[:, 0:1] + stats[:, 32:33], MASKED)
            total = jnp.where(live, stats[:, 64:65] + stats[:, 96:97], 0.0)
            parts.append((level, total, back[at, 0:8, :].astype(F32) * total))
        top = functools.reduce(jnp.maximum, [p[0] for p in parts])
        factors = [jnp.exp2(p[0] - top) for p in parts]
        total = sum(f * p[1] for f, p in zip(factors, parts))
        weighted = sum(f * p[2] for f, p in zip(factors, parts))
        out[j] = (weighted / total).astype(BF16)


def norm_kernel(mine, first, second, third, gain, residual, out):
    x = mine[...] + first[...].astype(F32) + second[...].astype(F32) + third[...].astype(F32)
    residual[...] = x
    spread = jnp.mean(x * x, axis=-1, keepdims=True)
    normed = (x * lax.rsqrt(spread + NORM_EPSILON) * gain[...]).astype(BF16)
    for g in range(out.shape[0]):
        out[g] = normed


def feed_kernel(x, gate, up, down, out):
    a = matmul_t(x[...], gate[...])
    b = matmul_t(x[...], up[...])
    hidden = (a / (1.0 + jnp.exp(-a)) * b).astype(BF16)
    width = 512
    for c in range(out.shape[1] // width):
        at = slice(c * width, (c + 1) * width)
        out[:, at] = matmul(hidden, down[:, at]).astype(BF16)


def total_kernel(table, arrived, kept, first, second, third):
    m = table[2]
    x = arrived[0].astype(F32)
    for g in range(1, arrived.shape[0]):
        x = x + arrived[g].astype(F32)
    for k, out in enumerate((kept, first, second, third)):
        rows = x[0:2]
        for c in range(1, 4):
            rows = jnp.where((m ^ k) == c, x[2 * c : 2 * c + 2], rows)
        out[...] = rows.astype(out.dtype)


def on_device(
    states,
    queries,
    new_keys,
    new_values,
    text_keys,
    text_values,
    text_length,
    image_keys,
    image_values,
    image_slot,
    block_list,
    block_count,
    image_first,
    image_count,
    out_weight,
    norm_gain,
    gate_weight,
    up_weight,
    down_weight,
):
    groups = lax.axis_size("group")
    depths = lax.axis_size("depth")
    ring = lax.axis_size("mp")
    mp_index = lax.axis_index("mp")
    ids = [lax.axis_index("group"), lax.axis_index("depth"), mp_index]
    table = jnp.concatenate(
        [jnp.stack(ids + [0] * 5).astype(jnp.int32), image_slot, block_list.reshape(-1)]
        + [block_count, image_first, image_count, text_length]
    )
    requests, heads, width = queries.shape
    half = requests // depths
    features = states.shape[1]

    routed = call(
        route_kernel,
        jax.ShapeDtypeStruct((groups, 16, width), BF16),
        [SMEM, VMEM],
        0,
        100_000,
        "route",
    )(table, queries)
    arrived = lax.all_to_all(routed, "group", 0, 0, tiled=True)

    part = jax.ShapeDtypeStruct((half, 16, width), F32)
    own, other = call(
        text_kernel,
        (part, part),
        [SMEM] + [VMEM] * 5,
        200_000_000,
        4_400_000,
        "text",
    )(table, queries, new_keys, new_values, text_keys, text_values)
    other = lax.ppermute(other, "depth", [(0, 1), (1, 0)])

    back = call(
        image_kernel,
        jax.ShapeDtypeStruct((groups, depths, 16, width), BF16),
        [VMEM] * 3,
        600_000_000,
        5_000_000,
        "image",
    )(arrived, image_keys, image_values)
    back = lax.all_to_all(
        back.reshape(groups * depths, 16, width), ("group", "depth"), 0, 0, tiled=True
    )
    attention = call(
        merge_kernel,
        jax.ShapeDtypeStruct((half, heads, width), BF16),
        [SMEM] + [VMEM] * 3,
        0,
        300_000,
        "merge",
    )(table, back, own, other)

    projected = jnp.dot(
        attention.reshape(half, heads * width), out_weight, preferred_element_type=F32
    )
    mine = lax.dynamic_update_slice_in_dim(
        jnp.zeros((half, features), F32), states.astype(F32), 2 * mp_index, 0
    )
    mine = projected + mine
    sent = mine.astype(BF16)
    passed = [
        lax.ppermute(sent, "mp", [(i, i ^ k) for i in range(ring)]) for k in range(1, ring)
    ]
    residual, normed = call(
        norm_kernel,
        (
            jax.ShapeDtypeStruct((half, features), F32),
            jax.ShapeDtypeStruct((groups, half, features), BF16),
        ),
        [VMEM] * 5,
        0,
        1_600_000,
        "norm",
    )(mine, *passed, norm_gain.reshape(1, features))
    tokens = lax.all_to_all(normed, "group", 0, 0, tiled=True).reshape(groups * half, features)
    down = call(
        feed_kernel,
        jax.ShapeDtypeStruct((groups * half, features), BF16),
        [VMEM] * 4,
        1_400_000_000,
        7_000_000,
        "feed",
    )(tokens, gate_weight.T, up_weight.T, down_weight)
    gathered = lax.all_to_all(down.reshape(groups, half, features), "group", 0, 0, tiled=True)
    pair = (2, features)
    kept, *sends = call(
        total_kernel,
        (jax.ShapeDtypeStruct(pair, F32),) + (jax.ShapeDtypeStruct(pair, BF16),) * 3,
        [SMEM, VMEM],
        0,
        1_300_000,
        "total",
    )(table, gathered)
    got = [
        lax.ppermute(s, "mp", [(i, i ^ k) for i in range(ring)])
        for k, s in zip(range(1, ring), sends)
    ]
    rest = lax.dynamic_slice_in_dim(residual, 2 * mp_index, 2, 0)
    for g in (kept, *got):
        rest = rest + g.astype(F32)
    return attention, rest.astype(BF16)


def solution(mesh):
    placed = (
        P(("group", "depth", "mp"), None),
        P("group", "mp", None),
        P("group", "mp", None),
        P("group", "mp", None),
        P("group", "mp", "depth", None),
        P("group", "mp", "depth", None),
        P("group"),
        P("group", "mp", None, None),
        P("group", "mp", None, None),
        P(),
        P(),
        P(),
        P("group"),
        P("group"),
        P("mp", None),
        P(),
        P(None, ("group", "mp")),
        P(None, ("group", "mp")),
        P(("group", "mp"), None),
    )
    return jax.shard_map(
        on_device,
        mesh=mesh,
        in_specs=placed,
        out_specs=(P(("group", "depth"), "mp", None), P(("group", "depth", "mp"), None)),
        check_vma=False,
    )
```

```python
import functools
import math

import jax
import jax.numpy as jnp
from jax import lax
from jax.experimental import pallas as pl
from jax.experimental.pallas import tpu as pltpu
from jax.sharding import PartitionSpec as P

MASKED = -1e30
NORM_EPSILON = 1e-05
BF16 = jnp.bfloat16
F32 = jnp.float32
VMEM = pl.BlockSpec(memory_space=pltpu.VMEM)
SMEM = pl.BlockSpec(memory_space=pltpu.SMEM)


HBM = pl.BlockSpec(memory_space=pltpu.MemorySpace.HBM)


def call(kernel, out_shape, in_specs, flops, nbytes, name, scratch=(), vmem=16 << 20, out_specs=None):
    return pl.pallas_call(
        kernel,
        out_shape=out_shape,
        in_specs=in_specs,
        out_specs=out_specs or jax.tree.map(lambda _: VMEM, out_shape),
        scratch_shapes=list(scratch),
        cost_estimate=pl.CostEstimate(flops=flops, bytes_accessed=nbytes, transcendentals=0),
        compiler_params=pltpu.CompilerParams(vmem_limit_bytes=vmem),
        name=name,
    )


def in_hbm(x):
    return pltpu.with_memory_space_constraint(x, pltpu.MemorySpace.HBM)


def matmul(a, b):
    return lax.dot_general(a, b, (((1,), (0,)), ((), ())), preferred_element_type=F32)


def matmul_t(a, b):
    return lax.dot_general(a, b, (((1,), (1,)), ((), ())), preferred_element_type=F32)


OWN_DEPTH, OWN_MP, LENGTH, SOURCE = 0, 1, 8, 24


def route_kernel(
    slots_hbm, blocks_hbm, count_hbm, first_hbm, images_hbm, lengths_hbm, queries_hbm, out, plan, *scratch
):
    slots, blocks, count, first, images, lengths, queries, sems = scratch
    copies = [
        pltpu.make_async_copy(src, dst, sems.at[k])
        for k, (src, dst) in enumerate(
            (
                (first_hbm, first),
                (images_hbm, images),
                (count_hbm, count),
                (blocks_hbm, blocks),
                (slots_hbm, slots),
                (lengths_hbm, lengths),
                (queries_hbm, queries),
            )
        )
    ]
    for copy in copies:
        copy.start()
    group, depth = lax.axis_index("group"), lax.axis_index("depth")
    requests = queries.shape[0]
    half = requests // 2
    out[...] = jnp.full(out.shape, -1.0, BF16)
    plan[OWN_DEPTH] = depth
    plan[OWN_MP] = lax.axis_index("mp")
    for copy in copies:
        copy.wait()
    listed = count[group]

    def source(place):
        slot = slots[blocks[group, jnp.minimum(place, blocks.shape[1] - 1)]]
        return slot >> 3, slot & 7

    for r in range(requests):
        start = first[r]
        skip = (start + depth) & 1
        place = start + skip
        owner, within = source(place)
        plan[LENGTH + r] = lengths[r]

        @pl.when((skip < images[r]) & (place < listed))
        def _():
            out[owner, 0:8, :] = queries[r]
            code = (within * 2 + r // half).astype(F32)
            out[owner, 8:16, :] = jnp.full((8, 128), code, F32).astype(BF16)

    for j in range(half):
        r = depth * half + j
        for k in range(2):
            place = first[r] + k
            owner, _ = source(place)
            live = (k < images[r]) & (place < listed)
            plan[SOURCE + 2 * j + k] = jnp.where(live, owner * 2 + (place & 1), -1)


def side_by_side(pair):
    return jnp.concatenate([pair[0], pair[1]], axis=1)


def text_kernel(plan, queries, new_keys, new_values, keys_hbm, values_hbm, own, other, keys, values, sems):
    depth = plan[OWN_DEPTH]
    requests, heads, width = queries.shape
    half = requests // 2
    span = keys.shape[2]
    step = requests // 4
    scale = 1.0 / (math.sqrt(width) * math.log(2.0))
    chunks = []
    for c in range(4):
        part, out = (depth, own) if c < 2 else (1 - depth, other)
        begin = part * half + (c % 2) * step
        at = pl.ds(begin, step)
        moves = [
            pltpu.make_async_copy(src.at[at], dst.at[at], sems.at[k, c])
            for k, (src, dst) in enumerate(((keys_hbm, keys), (values_hbm, values)))
        ]
        for move in moves:
            move.start()
        chunks.append((begin, (c % 2) * step, out, moves))
    low = lax.broadcasted_iota(jnp.int32, (heads, 1), 0) < heads // 2
    lane = lax.broadcasted_iota(jnp.int32, (heads, 128), 1)
    where = depth * span + lax.broadcasted_iota(jnp.int32, (heads, span), 1)
    for begin, row, out, moves in chunks:
        moves[0].wait()
        scores, fresh = [], []
        for j in range(step):
            r = begin + j
            q = queries[r]
            zero = jnp.zeros_like(q)
            both = jnp.concatenate([jnp.where(low, q, zero), jnp.where(low, zero, q)], axis=1)
            s = matmul_t(both, side_by_side(keys[r])) * scale
            scores.append(jnp.where(where < plan[LENGTH + r], s, MASKED))
            nk = new_keys[r].astype(F32)
            nk = jnp.where(low, nk[0:1], nk[1:2])
            fresh.append(jnp.sum(q.astype(F32) * nk, axis=-1, keepdims=True) * scale)
        s = jnp.concatenate(scores, axis=0)
        n = jnp.where(depth == 0, jnp.concatenate(fresh, axis=0), MASKED)
        level = jnp.floor(jnp.maximum(jnp.max(s, axis=-1, keepdims=True), n))
        w = jnp.where(s > 0.5 * MASKED, jnp.exp2(s - level), 0.0).astype(BF16)
        nw = jnp.where(n > 0.5 * MASKED, jnp.exp2(n - level), 0.0).astype(BF16).astype(F32)
        total = jnp.sum(w.astype(F32), axis=-1, keepdims=True) + nw
        moves[1].wait()
        for j in range(step):
            r = begin + j
            rows = slice(j * heads, (j + 1) * heads)
            o = matmul(w[rows], side_by_side(values[r]))
            o = jnp.where(low, o[:, 0:width], o[:, width : 2 * width])
            nv = new_values[r].astype(F32)
            o = o + nw[rows] * jnp.where(low, nv[0:1], nv[1:2])
            out[row + j, 0:8, :] = o
            out[row + j, 8:16, :] = jnp.where(lane < 64, level[rows], total[rows])


def image_kernel(arrived, keys, values, out):
    groups = arrived.shape[0]
    rows = groups * 8
    images, _, patches, width = keys.shape
    scale = 1.0 / (math.sqrt(width) * math.log(2.0))
    q = arrived[:, 0:8, :].reshape(rows, width)
    code = arrived[:, 8:16, :].reshape(rows, width).astype(F32)
    within = jnp.floor(code * 0.5)
    low = lax.broadcasted_iota(jnp.int32, (rows, 1), 0) % 8 < 4
    zero = jnp.zeros_like(q)
    both = jnp.concatenate([jnp.where(low, q, zero), jnp.where(low, zero, q)], axis=1)
    level = jnp.zeros((rows, 1), F32)
    total = jnp.zeros((rows, 1), F32)
    o = jnp.zeros((rows, 2 * width), F32)
    for i in range(images):
        mine = within[:, 0:1] == float(i)
        s = matmul_t(both, side_by_side(keys[i])) * scale
        here = jnp.floor(jnp.max(s, axis=-1, keepdims=True))
        w = jnp.where(mine, jnp.exp2(s - here), 0.0).astype(BF16)
        total = total + jnp.sum(w.astype(F32), axis=-1, keepdims=True)
        level = jnp.where(mine, here, level)
        o = o + matmul(w, side_by_side(values[i]))
    o = jnp.where(low, o[:, 0:width], o[:, width : 2 * width])
    o = o / jnp.where(total > 0.0, total, 1.0)
    lane = lax.broadcasted_iota(jnp.int32, (rows, width), 1)
    level_high = level.astype(BF16).astype(F32)
    total_high = total.astype(BF16).astype(F32)
    stats = jnp.where(
        lane < 64,
        jnp.where(lane < 32, level_high, level - level_high),
        jnp.where(lane < 96, total_high, total - total_high),
    )
    second = code - 2.0 * within
    o3 = o.astype(BF16).reshape(groups, 8, width)
    for h in range(2):
        out[:, h, 0:8, :] = o3
        out[:, h, 8:16, :] = (
            jnp.where(second == float(h), stats, 0.0).astype(BF16).reshape(groups, 8, width)
        )


def merge_kernel(plan, back, own, other, states, weight_hbm, out, mine, sent, joined, weight, sems):
    half, heads, width = out.shape
    pieces = sems.shape[0]
    depth = weight.shape[0] // pieces
    moves = [
        pltpu.make_async_copy(
            weight_hbm.at[pl.ds(k * depth, depth)], weight.at[pl.ds(k * depth, depth)], sems.at[k]
        )
        for k in range(pieces)
    ]
    for move in moves:
        move.start()
    rows = half * heads
    parts = []
    for ref in (own, other):
        stats = ref[:, 8:16, :].reshape(rows, 128)
        parts.append((stats[:, 0:1], stats[:, 64:65], ref[:, 0:8, :].reshape(rows, width)))
    lane = lax.broadcasted_iota(jnp.int32, (heads, 128), 1)
    dead = jnp.where(lane < 32, MASKED, 0.0)
    for k in range(2):
        stats, values = [], []
        for j in range(half):
            source = plan[SOURCE + 2 * j + k]
            at = jnp.maximum(source, 0)
            stats.append(jnp.where(source >= 0, back[at, 8:16, :].astype(F32), dead))
            values.append(back[at, 0:8, :].astype(F32))
        stats = jnp.concatenate(stats, axis=0)
        total = stats[:, 64:65] + stats[:, 96:97]
        parts.append(
            (stats[:, 0:1] + stats[:, 32:33], total, jnp.concatenate(values, axis=0) * total)
        )
    top = functools.reduce(jnp.maximum, [p[0] for p in parts])
    factors = [jnp.exp2(p[0] - top) for p in parts]
    total = sum(f * p[1] for f, p in zip(factors, parts))
    weighted = sum(f * p[2] for f, p in zip(factors, parts))
    value = weighted / total
    out[...] = value.astype(BF16).reshape(out.shape)
    joined[...] = value
    flat = jnp.concatenate(
        [joined[pl.ds(h, half, stride=heads), :] for h in range(heads)], axis=1
    ).astype(BF16)
    row = lax.broadcasted_iota(jnp.int32, (half, 1), 0) - 2 * plan[OWN_MP]
    step = 1024
    for k, move in enumerate(moves):
        move.wait()
        lhs = flat[:, k * depth : (k + 1) * depth]
        for c in range(mine.shape[1] // step):
            at = slice(c * step, (c + 1) * step)
            if k == 0:
                before = jnp.where(row == 1, states[1:2, at], states[0:1, at]).astype(F32)
                before = jnp.where((row == 0) | (row == 1), before, 0.0)
            else:
                before = mine[:, at]
            value = before + matmul(lhs, weight[k * depth : (k + 1) * depth, at])
            mine[:, at] = value
            if k == pieces - 1:
                sent[:, at] = value.astype(BF16)


def norm_kernel(plan, mine, first, second, third, gain, rest, out):
    x = mine[...] + first[...].astype(F32) + second[...].astype(F32) + third[...].astype(F32)
    kept = x[0:2]
    for c in range(1, x.shape[0] // 2):
        kept = jnp.where(plan[OWN_MP] == c, x[2 * c : 2 * c + 2], kept)
    rest[...] = kept
    spread = jnp.mean(x * x, axis=-1, keepdims=True)
    normed = (x * lax.rsqrt(spread + NORM_EPSILON) * gain[...]).astype(BF16)
    for g in range(out.shape[0]):
        out[g] = normed


def feed_kernel(x, gate, up, down, out, lined):
    a = matmul_t(x[...], gate[...])
    b = matmul_t(x[...], up[...])
    hidden = (a / (1.0 + jnp.exp(-a)) * b).astype(BF16)
    tokens = hidden.shape[0]
    tiles = lined.shape[0]
    for q in range(4):
        at = slice(q * tiles * 128, (q + 1) * tiles * 128)
        part = matmul(hidden, down[:, at])
        for c in range(tiles):
            lined[c, pl.ds(q, tokens, stride=4), :] = part[:, c * 128 : (c + 1) * 128]
    for c in range(tiles):
        block = lined[c].astype(BF16).reshape(out.shape[0], 8, 128)
        out[:, :, c * 128 : (c + 1) * 128] = block


def last_kernel(arrived, residual, out):
    total = arrived[0].astype(F32)
    for k in range(1, arrived.shape[0]):
        total = total + arrived[k].astype(F32)
    quarter = arrived.shape[2]
    for t in range(2):
        for q in range(4):
            at = slice(q * quarter, (q + 1) * quarter)
            row = t * 4 + q
            out[t : t + 1, at] = (residual[t : t + 1, at] + total[row : row + 1]).astype(BF16)


def on_device(
    states,
    queries,
    new_keys,
    new_values,
    text_keys,
    text_values,
    text_length,
    image_keys,
    image_values,
    image_slot,
    block_list,
    block_count,
    image_first,
    image_count,
    out_weight,
    norm_gain,
    gate_weight,
    up_weight,
    down_weight,
):
    groups = lax.axis_size("group")
    depths = lax.axis_size("depth")
    ring = lax.axis_size("mp")
    requests, heads, width = queries.shape
    half = requests // depths
    features = states.shape[1]

    integers = (image_slot, block_list, block_count, image_first, image_count, text_length)
    in_place = [in_hbm(x) for x in (*integers, queries)]
    routed, plan = call(
        route_kernel,
        (
            jax.ShapeDtypeStruct((groups, 16, width), BF16),
            jax.ShapeDtypeStruct((SOURCE + requests,), jnp.int32),
        ),
        [HBM] * 7,
        10_000_000_000,
        100_000,
        "route",
        scratch=[pltpu.SMEM(i.shape, jnp.int32) for i in integers]
        + [pltpu.VMEM(queries.shape, BF16), pltpu.SemaphoreType.DMA((len(in_place),))],
        out_specs=(VMEM, SMEM),
    )(*in_place)
    arrived = lax.all_to_all(routed, "group", 0, 0, tiled=True)

    part = jax.ShapeDtypeStruct((half, 16, width), F32)
    own, other = call(
        text_kernel,
        (part, part),
        [SMEM] + [VMEM] * 3 + [HBM] * 2,
        200_000_000,
        4_400_000,
        "text",
        scratch=[pltpu.VMEM(text_keys.shape, BF16), pltpu.VMEM(text_values.shape, BF16)]
        + [pltpu.SemaphoreType.DMA((2, 4))],
    )(plan, queries, new_keys, new_values, in_hbm(text_keys), in_hbm(text_values))
    other = lax.ppermute(other, "depth", [(0, 1), (1, 0)])

    back = call(
        image_kernel,
        jax.ShapeDtypeStruct((groups, depths, 16, width), BF16),
        [VMEM] * 3,
        600_000_000,
        5_000_000,
        "image",
    )(arrived, image_keys, image_values)
    back = lax.all_to_all(
        back.reshape(groups * depths, 16, width), ("group", "depth"), 0, 0, tiled=True
    )
    attention, mine, sent = call(
        merge_kernel,
        (
            jax.ShapeDtypeStruct((half, heads, width), BF16),
            jax.ShapeDtypeStruct((half, features), F32),
            jax.ShapeDtypeStruct((half, features), BF16),
        ),
        [SMEM] + [VMEM] * 4 + [HBM],
        100_000_000,
        8_800_000,
        "merge",
        scratch=[
            pltpu.VMEM((half * heads, width), F32),
            pltpu.VMEM(out_weight.shape, BF16),
            pltpu.SemaphoreType.DMA((4,)),
        ],
    )(plan, back, own, other, states, in_hbm(out_weight))
    passed = [
        lax.ppermute(sent, "mp", [(i, i ^ k) for i in range(ring)]) for k in range(1, ring)
    ]
    rest, normed = call(
        norm_kernel,
        (
            jax.ShapeDtypeStruct((2, features), F32),
            jax.ShapeDtypeStruct((groups, half, features), BF16),
        ),
        [SMEM] + [VMEM] * 5,
        10_000_000_000,
        1_600_000,
        "norm",
    )(plan, mine, *passed, norm_gain.reshape(1, features))
    tokens = lax.all_to_all(normed, "group", 0, 0, tiled=True).reshape(groups * half, features)
    peers = groups * ring
    down = call(
        feed_kernel,
        jax.ShapeDtypeStruct((peers, 8, features // 4), BF16),
        [VMEM] * 4,
        1_400_000_000,
        7_000_000,
        "feed",
        scratch=[pltpu.VMEM((features // 512, groups * half * 4, 128), F32)],
    )(tokens, gate_weight.T, up_weight.T, down_weight)
    gathered = lax.all_to_all(down, ("group", "mp"), 0, 0, tiled=True)
    layer_out = call(
        last_kernel,
        jax.ShapeDtypeStruct((2, features), BF16),
        [VMEM] * 2,
        0,
        1_300_000,
        "last",
    )(gathered, rest)
    return attention, layer_out


def solution(mesh):
    placed = (
        P(("group", "depth", "mp"), None),
        P("group", "mp", None),
        P("group", "mp", None),
        P("group", "mp", None),
        P("group", "mp", "depth", None),
        P("group", "mp", "depth", None),
        P("group"),
        P("group", "mp", None, None),
        P("group", "mp", None, None),
        P(),
        P(),
        P(),
        P("group"),
        P("group"),
        P("mp", None),
        P(),
        P(None, ("group", "mp")),
        P(None, ("group", "mp")),
        P(("group", "mp"), None),
    )
    return jax.shard_map(
        on_device,
        mesh=mesh,
        in_specs=placed,
        out_specs=(P(("group", "depth"), "mp", None), P(("group", "depth", "mp"), None)),
        check_vma=False,
    )
```

```python
import functools
import math

import jax
import jax.numpy as jnp
from jax import lax
from jax.experimental import pallas as pl
from jax.experimental.pallas import tpu as pltpu
from jax.sharding import PartitionSpec as P

MASKED = -1e30
NORM_EPSILON = 1e-05
BF16 = jnp.bfloat16
F32 = jnp.float32
VMEM = pl.BlockSpec(memory_space=pltpu.VMEM)
SMEM = pl.BlockSpec(memory_space=pltpu.SMEM)


HBM = pl.BlockSpec(memory_space=pltpu.MemorySpace.HBM)


def call(kernel, out_shape, in_specs, flops, nbytes, name, scratch=(), vmem=16 << 20, out_specs=None):
    return pl.pallas_call(
        kernel,
        out_shape=out_shape,
        in_specs=in_specs,
        out_specs=out_specs or jax.tree.map(lambda _: VMEM, out_shape),
        scratch_shapes=list(scratch),
        cost_estimate=pl.CostEstimate(flops=flops, bytes_accessed=nbytes, transcendentals=0),
        compiler_params=pltpu.CompilerParams(vmem_limit_bytes=vmem),
        name=name,
    )


def in_hbm(x):
    return pltpu.with_memory_space_constraint(x, pltpu.MemorySpace.HBM)


def matmul(a, b):
    return lax.dot_general(a, b, (((1,), (0,)), ((), ())), preferred_element_type=F32)


def matmul_t(a, b):
    return lax.dot_general(a, b, (((1,), (1,)), ((), ())), preferred_element_type=F32)


OWN_DEPTH, OWN_MP, LENGTH, SOURCE = 0, 1, 8, 24


def route_kernel(
    slots_hbm, blocks_hbm, count_hbm, first_hbm, images_hbm, lengths_hbm, queries_hbm, out, plan, *scratch
):
    slots, blocks, count, first, images, lengths, queries, sems = scratch
    copies = [
        pltpu.make_async_copy(src, dst, sems.at[k])
        for k, (src, dst) in enumerate(
            (
                (first_hbm, first),
                (images_hbm, images),
                (count_hbm, count),
                (blocks_hbm, blocks),
                (slots_hbm, slots),
                (lengths_hbm, lengths),
                (queries_hbm, queries),
            )
        )
    ]
    for copy in copies:
        copy.start()
    group, depth = lax.axis_index("group"), lax.axis_index("depth")
    requests = queries.shape[0]
    half = requests // 2
    out[...] = jnp.full(out.shape, -1.0, BF16)
    plan[OWN_DEPTH] = depth
    plan[OWN_MP] = lax.axis_index("mp")
    for copy in copies:
        copy.wait()
    listed = count[group]

    def source(place):
        slot = slots[blocks[group, jnp.minimum(place, blocks.shape[1] - 1)]]
        return slot >> 3, slot & 7

    for r in range(requests):
        start = first[r]
        skip = (start + depth) & 1
        place = start + skip
        owner, within = source(place)
        plan[LENGTH + r] = lengths[r]

        @pl.when((skip < images[r]) & (place < listed))
        def _():
            out[owner, 0:8, :] = queries[r]
            code = (within * 2 + r // half).astype(F32)
            out[owner, 8:16, :] = jnp.full((8, 128), code, F32).astype(BF16)

    for j in range(half):
        r = depth * half + j
        for k in range(2):
            place = first[r] + k
            owner, _ = source(place)
            live = (k < images[r]) & (place < listed)
            plan[SOURCE + 2 * j + k] = jnp.where(live, owner * 2 + (place & 1), -1)


def side_by_side(pair):
    return jnp.concatenate([pair[0], pair[1]], axis=1)


def text_kernel(plan, queries, new_keys, new_values, keys, values, own, other):
    depth = plan[OWN_DEPTH]
    requests, heads, width = queries.shape
    half = requests // 2
    span = keys.shape[2]
    step = requests // 4
    scale = 1.0 / (math.sqrt(width) * math.log(2.0))
    low = lax.broadcasted_iota(jnp.int32, (heads, 1), 0) < heads // 2
    lane = lax.broadcasted_iota(jnp.int32, (heads, 128), 1)
    where = depth * span + lax.broadcasted_iota(jnp.int32, (heads, span), 1)
    for c in range(4):
        part, out = (1 - depth, other) if c < 2 else (depth, own)
        row = (c % 2) * step
        begin = part * half + row
        scores, fresh = [], []
        for j in range(step):
            r = begin + j
            q = queries[r]
            zero = jnp.zeros_like(q)
            both = jnp.concatenate([jnp.where(low, q, zero), jnp.where(low, zero, q)], axis=1)
            s = matmul_t(both, side_by_side(keys[r])) * scale
            scores.append(jnp.where(where < plan[LENGTH + r], s, MASKED))
            nk = new_keys[r].astype(F32)
            nk = jnp.where(low, nk[0:1], nk[1:2])
            fresh.append(jnp.sum(q.astype(F32) * nk, axis=-1, keepdims=True) * scale)
        s = jnp.concatenate(scores, axis=0)
        n = jnp.where(depth == 0, jnp.concatenate(fresh, axis=0), MASKED)
        level = jnp.floor(jnp.maximum(jnp.max(s, axis=-1, keepdims=True), n))
        w = jnp.where(s > 0.5 * MASKED, jnp.exp2(s - level), 0.0).astype(BF16)
        nw = jnp.where(n > 0.5 * MASKED, jnp.exp2(n - level), 0.0).astype(BF16).astype(F32)
        total = jnp.sum(w.astype(F32), axis=-1, keepdims=True) + nw
        for j in range(step):
            r = begin + j
            rows = slice(j * heads, (j + 1) * heads)
            o = matmul(w[rows], side_by_side(values[r]))
            o = jnp.where(low, o[:, 0:width], o[:, width : 2 * width])
            nv = new_values[r].astype(F32)
            o = o + nw[rows] * jnp.where(low, nv[0:1], nv[1:2])
            out[row + j, 0:8, :] = o
            out[row + j, 8:16, :] = jnp.where(lane < 64, level[rows], total[rows])


def image_kernel(after, arrived, keys, values, out):
    del after
    groups = arrived.shape[0]
    rows = groups * 8
    images, _, patches, width = keys.shape
    scale = 1.0 / (math.sqrt(width) * math.log(2.0))
    q = arrived[:, 0:8, :].reshape(rows, width)
    code = arrived[:, 8:16, :].reshape(rows, width).astype(F32)
    within = jnp.floor(code * 0.5)
    low = lax.broadcasted_iota(jnp.int32, (rows, 1), 0) % 8 < 4
    zero = jnp.zeros_like(q)
    both = jnp.concatenate([jnp.where(low, q, zero), jnp.where(low, zero, q)], axis=1)
    level = jnp.zeros((rows, 1), F32)
    total = jnp.zeros((rows, 1), F32)
    o = jnp.zeros((rows, 2 * width), F32)
    for i in range(images):
        mine = within[:, 0:1] == float(i)
        s = matmul_t(both, side_by_side(keys[i])) * scale
        here = jnp.floor(jnp.max(s, axis=-1, keepdims=True))
        w = jnp.where(mine, jnp.exp2(s - here), 0.0).astype(BF16)
        total = total + jnp.sum(w.astype(F32), axis=-1, keepdims=True)
        level = jnp.where(mine, here, level)
        o = o + matmul(w, side_by_side(values[i]))
    o = jnp.where(low, o[:, 0:width], o[:, width : 2 * width])
    o = o / jnp.where(total > 0.0, total, 1.0)
    lane = lax.broadcasted_iota(jnp.int32, (rows, width), 1)
    level_high = level.astype(BF16).astype(F32)
    total_high = total.astype(BF16).astype(F32)
    stats = jnp.where(
        lane < 64,
        jnp.where(lane < 32, level_high, level - level_high),
        jnp.where(lane < 96, total_high, total - total_high),
    )
    second = code - 2.0 * within
    o3 = o.astype(BF16).reshape(groups, 8, width)
    for h in range(2):
        out[:, h, 0:8, :] = o3
        out[:, h, 8:16, :] = (
            jnp.where(second == float(h), stats, 0.0).astype(BF16).reshape(groups, 8, width)
        )


def merge_kernel(plan, back, own, other, states, weight, out, mine, sent, joined):
    half, heads, width = out.shape
    rows = half * heads
    parts = []
    for ref in (own, other):
        stats = ref[:, 8:16, :].reshape(rows, 128)
        parts.append((stats[:, 0:1], stats[:, 64:65], ref[:, 0:8, :].reshape(rows, width)))
    lane = lax.broadcasted_iota(jnp.int32, (heads, 128), 1)
    dead = jnp.where(lane < 32, MASKED, 0.0)
    for k in range(2):
        stats, values = [], []
        for j in range(half):
            source = plan[SOURCE + 2 * j + k]
            at = jnp.maximum(source, 0)
            stats.append(jnp.where(source >= 0, back[at, 8:16, :].astype(F32), dead))
            values.append(back[at, 0:8, :].astype(F32))
        stats = jnp.concatenate(stats, axis=0)
        total = stats[:, 64:65] + stats[:, 96:97]
        parts.append(
            (stats[:, 0:1] + stats[:, 32:33], total, jnp.concatenate(values, axis=0) * total)
        )
    top = functools.reduce(jnp.maximum, [p[0] for p in parts])
    factors = [jnp.exp2(p[0] - top) for p in parts]
    total = sum(f * p[1] for f, p in zip(factors, parts))
    weighted = sum(f * p[2] for f, p in zip(factors, parts))
    value = weighted / total
    out[...] = value.astype(BF16).reshape(out.shape)
    joined[...] = value
    flat = jnp.concatenate(
        [joined[pl.ds(h, half, stride=heads), :] for h in range(heads)], axis=1
    ).astype(BF16)
    row = lax.broadcasted_iota(jnp.int32, (half, 1), 0) - 2 * plan[OWN_MP]
    step = 512
    for c in range(mine.shape[1] // step):
        at = slice(c * step, (c + 1) * step)
        before = jnp.where(row == 1, states[1:2, at], states[0:1, at]).astype(F32)
        before = jnp.where((row == 0) | (row == 1), before, 0.0)
        value = before + matmul(flat, weight[:, at])
        mine[:, at] = value
        sent[:, at] = value.astype(BF16)


def norm_kernel(plan, mine, first, second, third, gain, rest, out):
    x = mine[...] + first[...].astype(F32) + second[...].astype(F32) + third[...].astype(F32)
    kept = x[0:2]
    for c in range(1, x.shape[0] // 2):
        kept = jnp.where(plan[OWN_MP] == c, x[2 * c : 2 * c + 2], kept)
    rest[...] = kept
    spread = jnp.mean(x * x, axis=-1, keepdims=True)
    normed = (x * lax.rsqrt(spread + NORM_EPSILON) * gain[...]).astype(BF16)
    for g in range(out.shape[0]):
        out[g] = normed


def feed_kernel(x, gate, up, down, out, lined):
    a = matmul_t(x[...], gate[...])
    b = matmul_t(x[...], up[...])
    hidden = (a / (1.0 + jnp.exp(-a)) * b).astype(BF16)
    tokens = hidden.shape[0]
    tiles = lined.shape[0]
    for q in range(4):
        at = slice(q * tiles * 128, (q + 1) * tiles * 128)
        part = matmul(hidden, down[:, at])
        for c in range(tiles):
            lined[c, pl.ds(q, tokens, stride=4), :] = part[:, c * 128 : (c + 1) * 128]
    for c in range(tiles):
        block = lined[c].astype(BF16).reshape(out.shape[0], 8, 128)
        out[:, :, c * 128 : (c + 1) * 128] = block


def last_kernel(arrived, residual, out):
    total = arrived[0].astype(F32)
    for k in range(1, arrived.shape[0]):
        total = total + arrived[k].astype(F32)
    quarter = arrived.shape[2]
    for t in range(2):
        for q in range(4):
            at = slice(q * quarter, (q + 1) * quarter)
            row = t * 4 + q
            out[t : t + 1, at] = (residual[t : t + 1, at] + total[row : row + 1]).astype(BF16)


def on_device(
    states,
    queries,
    new_keys,
    new_values,
    text_keys,
    text_values,
    text_length,
    image_keys,
    image_values,
    image_slot,
    block_list,
    block_count,
    image_first,
    image_count,
    out_weight,
    norm_gain,
    gate_weight,
    up_weight,
    down_weight,
):
    groups = lax.axis_size("group")
    depths = lax.axis_size("depth")
    ring = lax.axis_size("mp")
    requests, heads, width = queries.shape
    half = requests // depths
    features = states.shape[1]

    integers = (image_slot, block_list, block_count, image_first, image_count, text_length)
    in_place = [in_hbm(x) for x in (*integers, queries)]
    routed, plan = call(
        route_kernel,
        (
            jax.ShapeDtypeStruct((groups, 16, width), BF16),
            jax.ShapeDtypeStruct((SOURCE + requests,), jnp.int32),
        ),
        [HBM] * 7,
        20_000_000_000,
        100_000,
        "route",
        scratch=[pltpu.SMEM(i.shape, jnp.int32) for i in integers]
        + [pltpu.VMEM(queries.shape, BF16), pltpu.SemaphoreType.DMA((len(in_place),))],
        out_specs=(VMEM, SMEM),
    )(*in_place)
    arrived = lax.all_to_all(routed, "group", 0, 0, tiled=True)
    arrived, plan = lax.optimization_barrier((arrived, plan))

    part = jax.ShapeDtypeStruct((half, 16, width), F32)
    own, other = call(
        text_kernel,
        (part, part),
        [SMEM] + [VMEM] * 5,
        200_000_000,
        4_400_000,
        "text",
    )(plan, queries, new_keys, new_values, text_keys, text_values)
    other = lax.ppermute(other, "depth", [(0, 1), (1, 0)])

    back = call(
        image_kernel,
        jax.ShapeDtypeStruct((groups, depths, 16, width), BF16),
        [VMEM] * 4,
        10_000_000_000,
        5_000_000,
        "image",
    )(own, arrived, image_keys, image_values)
    back, other = lax.optimization_barrier((back, other))
    back = lax.all_to_all(
        back.reshape(groups * depths, 16, width), ("group", "depth"), 0, 0, tiled=True
    )
    attention, mine, sent = call(
        merge_kernel,
        (
            jax.ShapeDtypeStruct((half, heads, width), BF16),
            jax.ShapeDtypeStruct((half, features), F32),
            jax.ShapeDtypeStruct((half, features), BF16),
        ),
        [SMEM] + [VMEM] * 5,
        100_000_000,
        8_800_000,
        "merge",
        scratch=[pltpu.VMEM((half * heads, width), F32)],
    )(plan, back, own, other, states, out_weight)
    passed = [
        lax.ppermute(sent, "mp", [(i, i ^ k) for i in range(ring)]) for k in range(1, ring)
    ]
    rest, normed = call(
        norm_kernel,
        (
            jax.ShapeDtypeStruct((2, features), F32),
            jax.ShapeDtypeStruct((groups, half, features), BF16),
        ),
        [SMEM] + [VMEM] * 5,
        10_000_000_000,
        1_600_000,
        "norm",
    )(plan, mine, *passed, norm_gain.reshape(1, features))
    tokens = lax.all_to_all(normed, "group", 0, 0, tiled=True).reshape(groups * half, features)
    peers = groups * ring
    down = call(
        feed_kernel,
        jax.ShapeDtypeStruct((peers, 8, features // 4), BF16),
        [VMEM] * 4,
        1_400_000_000,
        7_000_000,
        "feed",
        scratch=[pltpu.VMEM((features // 512, groups * half * 4, 128), F32)],
    )(tokens, gate_weight.T, up_weight.T, down_weight)
    gathered = lax.all_to_all(down, ("group", "mp"), 0, 0, tiled=True)
    layer_out = call(
        last_kernel,
        jax.ShapeDtypeStruct((2, features), BF16),
        [VMEM] * 2,
        0,
        1_300_000,
        "last",
    )(gathered, rest)
    return attention, layer_out


def solution(mesh):
    placed = (
        P(("group", "depth", "mp"), None),
        P("group", "mp", None),
        P("group", "mp", None),
        P("group", "mp", None),
        P("group", "mp", "depth", None),
        P("group", "mp", "depth", None),
        P("group"),
        P("group", "mp", None, None),
        P("group", "mp", None, None),
        P(),
        P(),
        P(),
        P("group"),
        P("group"),
        P("mp", None),
        P(),
        P(None, ("group", "mp")),
        P(None, ("group", "mp")),
        P(("group", "mp"), None),
    )
    return jax.shard_map(
        on_device,
        mesh=mesh,
        in_specs=placed,
        out_specs=(P(("group", "depth"), "mp", None), P(("group", "depth", "mp"), None)),
        check_vma=False,
    )
```

```python
import functools
import math

import jax
import jax.numpy as jnp
from jax import lax
from jax.experimental import pallas as pl
from jax.experimental.pallas import tpu as pltpu
from jax.sharding import PartitionSpec as P

MASKED = -1e30
NORM_EPSILON = 1e-05
BF16 = jnp.bfloat16
F32 = jnp.float32
VMEM = pl.BlockSpec(memory_space=pltpu.VMEM)
SMEM = pl.BlockSpec(memory_space=pltpu.SMEM)


HBM = pl.BlockSpec(memory_space=pltpu.MemorySpace.HBM)


def call(kernel, out_shape, in_specs, flops, nbytes, name, scratch=(), vmem=16 << 20, out_specs=None):
    return pl.pallas_call(
        kernel,
        out_shape=out_shape,
        in_specs=in_specs,
        out_specs=out_specs or jax.tree.map(lambda _: VMEM, out_shape),
        scratch_shapes=list(scratch),
        cost_estimate=pl.CostEstimate(flops=flops, bytes_accessed=nbytes, transcendentals=0),
        compiler_params=pltpu.CompilerParams(vmem_limit_bytes=vmem),
        name=name,
    )


def in_hbm(x):
    return pltpu.with_memory_space_constraint(x, pltpu.MemorySpace.HBM)


def matmul(a, b):
    return lax.dot_general(a, b, (((1,), (0,)), ((), ())), preferred_element_type=F32)


def matmul_t(a, b):
    return lax.dot_general(a, b, (((1,), (1,)), ((), ())), preferred_element_type=F32)


OWN_DEPTH, OWN_MP, LENGTH, SOURCE = 0, 1, 8, 24


def route_kernel(
    slots_hbm, blocks_hbm, count_hbm, first_hbm, images_hbm, lengths_hbm, queries_hbm, out, plan, *scratch
):
    slots, blocks, count, first, images, lengths, queries, sems = scratch
    copies = [
        pltpu.make_async_copy(src, dst, sems.at[k])
        for k, (src, dst) in enumerate(
            (
                (first_hbm, first),
                (images_hbm, images),
                (count_hbm, count),
                (blocks_hbm, blocks),
                (slots_hbm, slots),
                (lengths_hbm, lengths),
                (queries_hbm, queries),
            )
        )
    ]
    for copy in copies:
        copy.start()
    group, depth = lax.axis_index("group"), lax.axis_index("depth")
    requests = queries.shape[0]
    half = requests // 2
    out[...] = jnp.full(out.shape, -1.0, BF16)
    plan[OWN_DEPTH] = depth
    plan[OWN_MP] = lax.axis_index("mp")
    for copy in copies:
        copy.wait()
    listed = count[group]

    def source(place):
        slot = slots[blocks[group, jnp.minimum(place, blocks.shape[1] - 1)]]
        return slot >> 3, slot & 7

    for r in range(requests):
        start, read = first[r], images[r]
        plan[LENGTH + r] = lengths[r]
        for k in range(2):
            place = start + k
            owner, within = source(place)
            live = (k < read) & (place < listed)
            plan[SOURCE + 2 * r + k] = jnp.where(live, owner * 2 + (place & 1), -1)

            @pl.when(live & ((place & 1) == depth))
            def _():
                out[owner, 0:8, :] = queries[r]
                code = (within * 2 + r // half).astype(F32)
                out[owner, 8:16, :] = jnp.full((8, 128), code, F32).astype(BF16)


def side_by_side(pair):
    return jnp.concatenate([pair[0], pair[1]], axis=1)


def text_kernel(plan, queries, new_keys, new_values, keys, values, own, other):
    depth = plan[OWN_DEPTH]
    requests, heads, width = queries.shape
    half = requests // 2
    rows = requests * heads
    span = keys.shape[2]
    scale = 1.0 / (math.sqrt(width) * math.log(2.0))
    order = [(p + half * depth) % requests for p in range(requests)]
    low8 = lax.broadcasted_iota(jnp.int32, (heads, 1), 0) < heads // 2
    low = lax.broadcasted_iota(jnp.int32, (rows, 1), 0) % heads < heads // 2
    lane = lax.broadcasted_iota(jnp.int32, (1, rows), 1) // heads
    q = jnp.concatenate([queries[r] for r in order], axis=0)
    zero = jnp.zeros_like(q)
    both = jnp.concatenate([jnp.where(low, q, zero), jnp.where(low, zero, q)], axis=1)
    across = jnp.zeros((span, rows), F32)
    for p, r in enumerate(order):
        across = jnp.where(lane == p, matmul_t(side_by_side(keys[r]), both), across)
    length = jnp.concatenate([jnp.full((heads, 1), plan[LENGTH + r]) for r in order], axis=0)
    where = depth * span + lax.broadcasted_iota(jnp.int32, (rows, span), 1)
    allowed = where < length
    s = jnp.where(allowed, across.T * scale, MASKED)

    def per_head(ref):
        pairs = [ref[r].astype(F32) for r in order]
        return jnp.concatenate([jnp.where(low8, x[0:1], x[1:2]) for x in pairs], axis=0)

    fresh = jnp.sum(q.astype(F32) * per_head(new_keys), axis=-1, keepdims=True) * scale
    n = jnp.where(depth == 0, fresh, MASKED)
    level = jnp.floor(jnp.maximum(jnp.max(s, axis=-1, keepdims=True), n))
    w = jnp.where(allowed, jnp.exp2(s - level), 0.0).astype(BF16)
    nw = jnp.where(depth == 0, jnp.exp2(n - level), 0.0).astype(BF16).astype(F32)
    total = jnp.sum(w.astype(F32), axis=-1, keepdims=True) + nw
    added = nw * per_head(new_values)
    column = lax.broadcasted_iota(jnp.int32, (rows, 128), 1)
    stats = jnp.where(column < 64, level, total)
    for p, r in enumerate(order):
        at = slice(p * heads, (p + 1) * heads)
        o = matmul(w[at], side_by_side(values[r]))
        out = own if p < half else other
        out[p % half, 0:8, :] = jnp.where(low8, o[:, 0:width], o[:, width : 2 * width]) + added[at]
        out[p % half, 8:16, :] = stats[at]


def image_kernel(after, arrived, keys, values, out):
    del after
    groups = arrived.shape[0]
    rows = groups * 8
    images, _, patches, width = keys.shape
    scale = 1.0 / (math.sqrt(width) * math.log(2.0))
    q = arrived[:, 0:8, :].reshape(rows, width)
    code = arrived[:, 8:16, :].reshape(rows, width).astype(F32)
    within = jnp.floor(code * 0.5)
    within_lane = within.T[0:1, :]
    low = lax.broadcasted_iota(jnp.int32, (rows, 1), 0) % 8 < 4
    zero = jnp.zeros_like(q)
    both = jnp.concatenate([jnp.where(low, q, zero), jnp.where(low, zero, q)], axis=1)
    across = jnp.zeros((patches, rows), F32)
    for i in range(images):
        across = jnp.where(
            within_lane == float(i), matmul_t(side_by_side(keys[i]), both), across
        )
    s = across.T * scale
    level = jnp.floor(jnp.max(s, axis=-1, keepdims=True))
    w = jnp.exp2(s - level).astype(BF16)
    present = within[:, 0:1] >= 0.0
    total = jnp.where(present, jnp.sum(w.astype(F32), axis=-1, keepdims=True), 0.0)
    nothing = jnp.zeros_like(w)
    o = jnp.zeros((rows, 2 * width), F32)
    for i in range(images):
        o = o + matmul(jnp.where(within[:, 0:1] == float(i), w, nothing), side_by_side(values[i]))
    o = jnp.where(low, o[:, 0:width], o[:, width : 2 * width])
    o = o / jnp.where(present, total, 1.0)
    lane = lax.broadcasted_iota(jnp.int32, (rows, width), 1)
    level_high = level.astype(BF16).astype(F32)
    total_high = total.astype(BF16).astype(F32)
    stats = jnp.where(
        lane < 64,
        jnp.where(lane < 32, level_high, level - level_high),
        jnp.where(lane < 96, total_high, total - total_high),
    )
    second = code - 2.0 * within
    o3 = o.astype(BF16).reshape(groups, 8, width)
    for h in range(2):
        out[:, h, 0:8, :] = o3
        out[:, h, 8:16, :] = (
            jnp.where(second == float(h), stats, 0.0).astype(BF16).reshape(groups, 8, width)
        )


def merge_kernel(plan, back, own, other, states, weight, out, mine, sent, joined):
    half, heads, width = out.shape
    rows = half * heads
    parts = []
    for ref in (own, other):
        stats = ref[:, 8:16, :].reshape(rows, 128)
        parts.append((stats[:, 0:1], stats[:, 64:65], ref[:, 0:8, :].reshape(rows, width)))
    lane = lax.broadcasted_iota(jnp.int32, (heads, 128), 1)
    dead = jnp.where(lane < 32, MASKED, 0.0)
    for k in range(2):
        stats, values = [], []
        for j in range(half):
            source = plan[SOURCE + 2 * (plan[OWN_DEPTH] * half + j) + k]
            at = jnp.maximum(source, 0)
            stats.append(jnp.where(source >= 0, back[at, 8:16, :].astype(F32), dead))
            values.append(back[at, 0:8, :].astype(F32))
        stats = jnp.concatenate(stats, axis=0)
        total = stats[:, 64:65] + stats[:, 96:97]
        parts.append(
            (stats[:, 0:1] + stats[:, 32:33], total, jnp.concatenate(values, axis=0) * total)
        )
    top = functools.reduce(jnp.maximum, [p[0] for p in parts])
    factors = [jnp.exp2(p[0] - top) for p in parts]
    total = sum(f * p[1] for f, p in zip(factors, parts))
    weighted = sum(f * p[2] for f, p in zip(factors, parts))
    value = weighted / total
    out[...] = value.astype(BF16).reshape(out.shape)
    joined[...] = value
    flat = jnp.concatenate(
        [joined[pl.ds(h, half, stride=heads), :] for h in range(heads)], axis=1
    ).astype(BF16)
    row = lax.broadcasted_iota(jnp.int32, (half, 1), 0) - 2 * plan[OWN_MP]
    step = 512
    for c in range(mine.shape[1] // step):
        at = slice(c * step, (c + 1) * step)
        before = jnp.where(row == 1, states[1:2, at], states[0:1, at]).astype(F32)
        before = jnp.where((row == 0) | (row == 1), before, 0.0)
        value = before + matmul(flat, weight[:, at])
        mine[:, at] = value
        sent[:, at] = value.astype(BF16)


def norm_kernel(plan, mine, first, second, third, gain, rest, out):
    x = mine[...] + first[...].astype(F32) + second[...].astype(F32) + third[...].astype(F32)
    kept = x[0:2]
    for c in range(1, x.shape[0] // 2):
        kept = jnp.where(plan[OWN_MP] == c, x[2 * c : 2 * c + 2], kept)
    rest[...] = kept
    spread = jnp.mean(x * x, axis=-1, keepdims=True)
    normed = (x * lax.rsqrt(spread + NORM_EPSILON) * gain[...]).astype(BF16)
    for g in range(out.shape[0]):
        out[g] = normed


def feed_kernel(x, gate, up, down, out, lined):
    a = matmul_t(x[...], gate[...])
    b = matmul_t(x[...], up[...])
    hidden = (a / (1.0 + jnp.exp(-a)) * b).astype(BF16)
    tokens = hidden.shape[0]
    tiles = lined.shape[0]
    for q in range(4):
        at = slice(q * tiles * 128, (q + 1) * tiles * 128)
        part = matmul(hidden, down[:, at])
        for c in range(tiles):
            lined[c, pl.ds(q, tokens, stride=4), :] = part[:, c * 128 : (c + 1) * 128]
    for c in range(tiles):
        block = lined[c].astype(BF16).reshape(out.shape[0], 8, 128)
        out[:, :, c * 128 : (c + 1) * 128] = block


def last_kernel(arrived, residual, out):
    total = arrived[0].astype(F32)
    for k in range(1, arrived.shape[0]):
        total = total + arrived[k].astype(F32)
    quarter = arrived.shape[2]
    for t in range(2):
        for q in range(4):
            at = slice(q * quarter, (q + 1) * quarter)
            row = t * 4 + q
            out[t : t + 1, at] = (residual[t : t + 1, at] + total[row : row + 1]).astype(BF16)


def on_device(
    states,
    queries,
    new_keys,
    new_values,
    text_keys,
    text_values,
    text_length,
    image_keys,
    image_values,
    image_slot,
    block_list,
    block_count,
    image_first,
    image_count,
    out_weight,
    norm_gain,
    gate_weight,
    up_weight,
    down_weight,
):
    groups = lax.axis_size("group")
    depths = lax.axis_size("depth")
    ring = lax.axis_size("mp")
    requests, heads, width = queries.shape
    half = requests // depths
    features = states.shape[1]

    integers = (image_slot, block_list, block_count, image_first, image_count, text_length)
    in_place = [in_hbm(x) for x in (*integers, queries)]
    routed, plan = call(
        route_kernel,
        (
            jax.ShapeDtypeStruct((groups, 16, width), BF16),
            jax.ShapeDtypeStruct((SOURCE + 2 * requests,), jnp.int32),
        ),
        [HBM] * 7,
        20_000_000_000,
        100_000,
        "route",
        scratch=[pltpu.SMEM(i.shape, jnp.int32) for i in integers]
        + [pltpu.VMEM(queries.shape, BF16), pltpu.SemaphoreType.DMA((len(in_place),))],
        out_specs=(VMEM, SMEM),
    )(*in_place)
    arrived = lax.all_to_all(routed, "group", 0, 0, tiled=True)
    arrived, plan = lax.optimization_barrier((arrived, plan))

    part = jax.ShapeDtypeStruct((half, 16, width), F32)
    own, other = call(
        text_kernel,
        (part, part),
        [SMEM] + [VMEM] * 5,
        200_000_000,
        4_400_000,
        "text",
    )(plan, queries, new_keys, new_values, text_keys, text_values)
    other = lax.ppermute(other, "depth", [(0, 1), (1, 0)])

    back = call(
        image_kernel,
        jax.ShapeDtypeStruct((groups, depths, 16, width), BF16),
        [VMEM] * 4,
        10_000_000_000,
        5_000_000,
        "image",
    )(own, arrived, image_keys, image_values)
    back, other = lax.optimization_barrier((back, other))
    back = lax.all_to_all(
        back.reshape(groups * depths, 16, width), ("group", "depth"), 0, 0, tiled=True
    )
    attention, mine, sent = call(
        merge_kernel,
        (
            jax.ShapeDtypeStruct((half, heads, width), BF16),
            jax.ShapeDtypeStruct((half, features), F32),
            jax.ShapeDtypeStruct((half, features), BF16),
        ),
        [SMEM] + [VMEM] * 5,
        100_000_000,
        8_800_000,
        "merge",
        scratch=[pltpu.VMEM((half * heads, width), F32)],
    )(plan, back, own, other, states, out_weight)
    passed = [
        lax.ppermute(sent, "mp", [(i, i ^ k) for i in range(ring)]) for k in range(1, ring)
    ]
    rest, normed = call(
        norm_kernel,
        (
            jax.ShapeDtypeStruct((2, features), F32),
            jax.ShapeDtypeStruct((groups, half, features), BF16),
        ),
        [SMEM] + [VMEM] * 5,
        10_000_000_000,
        1_600_000,
        "norm",
    )(plan, mine, *passed, norm_gain.reshape(1, features))
    tokens = lax.all_to_all(normed, "group", 0, 0, tiled=True).reshape(groups * half, features)
    peers = groups * ring
    down = call(
        feed_kernel,
        jax.ShapeDtypeStruct((peers, 8, features // 4), BF16),
        [VMEM] * 4,
        1_400_000_000,
        7_000_000,
        "feed",
        scratch=[pltpu.VMEM((features // 512, groups * half * 4, 128), F32)],
    )(tokens, gate_weight.T, up_weight.T, down_weight)
    gathered = lax.all_to_all(down, ("group", "mp"), 0, 0, tiled=True)
    layer_out = call(
        last_kernel,
        jax.ShapeDtypeStruct((2, features), BF16),
        [VMEM] * 2,
        0,
        1_300_000,
        "last",
    )(gathered, rest)
    return attention, layer_out


def solution(mesh):
    placed = (
        P(("group", "depth", "mp"), None),
        P("group", "mp", None),
        P("group", "mp", None),
        P("group", "mp", None),
        P("group", "mp", "depth", None),
        P("group", "mp", "depth", None),
        P("group"),
        P("group", "mp", None, None),
        P("group", "mp", None, None),
        P(),
        P(),
        P(),
        P("group"),
        P("group"),
        P("mp", None),
        P(),
        P(None, ("group", "mp")),
        P(None, ("group", "mp")),
        P(("group", "mp"), None),
    )
    return jax.shard_map(
        on_device,
        mesh=mesh,
        in_specs=placed,
        out_specs=(P(("group", "depth"), "mp", None), P(("group", "depth", "mp"), None)),
        check_vma=False,
    )
```

```python
import functools
import math

import jax
import jax.numpy as jnp
from jax import lax
from jax.experimental import pallas as pl
from jax.experimental.pallas import tpu as pltpu
from jax.sharding import PartitionSpec as P

MASKED = -1e30
NORM_EPSILON = 1e-05
BF16 = jnp.bfloat16
F32 = jnp.float32
VMEM = pl.BlockSpec(memory_space=pltpu.VMEM)
SMEM = pl.BlockSpec(memory_space=pltpu.SMEM)


HBM = pl.BlockSpec(memory_space=pltpu.MemorySpace.HBM)


def call(kernel, out_shape, in_specs, flops, nbytes, name, scratch=(), vmem=16 << 20, out_specs=None):
    return pl.pallas_call(
        kernel,
        out_shape=out_shape,
        in_specs=in_specs,
        out_specs=out_specs or jax.tree.map(lambda _: VMEM, out_shape),
        scratch_shapes=list(scratch),
        cost_estimate=pl.CostEstimate(flops=flops, bytes_accessed=nbytes, transcendentals=0),
        compiler_params=pltpu.CompilerParams(vmem_limit_bytes=vmem),
        name=name,
    )


def in_hbm(x):
    return pltpu.with_memory_space_constraint(x, pltpu.MemorySpace.HBM)


def matmul(a, b):
    return lax.dot_general(a, b, (((1,), (0,)), ((), ())), preferred_element_type=F32)


def matmul_t(a, b):
    return lax.dot_general(a, b, (((1,), (1,)), ((), ())), preferred_element_type=F32)


OWN_DEPTH, OWN_MP, LENGTH, SOURCE = 0, 1, 8, 24


def route_kernel(
    slots_hbm, blocks_hbm, count_hbm, first_hbm, images_hbm, lengths_hbm, queries_hbm, out, plan, *scratch
):
    slots, blocks, count, first, images, lengths, queries, sems = scratch
    copies = [
        pltpu.make_async_copy(src, dst, sems.at[k])
        for k, (src, dst) in enumerate(
            (
                (first_hbm, first),
                (images_hbm, images),
                (count_hbm, count),
                (blocks_hbm, blocks),
                (slots_hbm, slots),
                (lengths_hbm, lengths),
                (queries_hbm, queries),
            )
        )
    ]
    for copy in copies:
        copy.start()
    group, depth = lax.axis_index("group"), lax.axis_index("depth")
    requests = queries.shape[0]
    half = requests // 2
    out[...] = jnp.full(out.shape, -1.0, BF16)
    plan[OWN_DEPTH] = depth
    plan[OWN_MP] = lax.axis_index("mp")
    for copy in copies:
        copy.wait()
    listed = count[group]

    def source(place):
        slot = slots[blocks[group, jnp.minimum(place, blocks.shape[1] - 1)]]
        return slot >> 3, slot & 7

    for r in range(requests):
        start, read = first[r], images[r]
        plan[LENGTH + r] = lengths[r]
        for k in range(2):
            place = start + k
            owner, within = source(place)
            live = (k < read) & (place < listed)
            plan[SOURCE + 2 * r + k] = jnp.where(live, owner * 2 + (place & 1), -1)

            @pl.when(live & ((place & 1) == depth))
            def _():
                out[owner, 0:8, :] = queries[r]
                code = (within * 2 + r // half).astype(F32)
                out[owner, 8:16, :] = jnp.full((8, 128), code, F32).astype(BF16)


def side_by_side(pair):
    return jnp.concatenate([pair[0], pair[1]], axis=1)


def text_kernel(plan, queries, new_keys, new_values, keys, values, own, other):
    depth = plan[OWN_DEPTH]
    requests, heads, width = queries.shape
    half = requests // 2
    rows = requests * heads
    span = keys.shape[2]
    scale = 1.0 / (math.sqrt(width) * math.log(2.0))
    order = [(p + half * depth) % requests for p in range(requests)]
    low8 = lax.broadcasted_iota(jnp.int32, (heads, 1), 0) < heads // 2
    low = lax.broadcasted_iota(jnp.int32, (rows, 1), 0) % heads < heads // 2
    lane = lax.broadcasted_iota(jnp.int32, (1, rows), 1) // heads
    q = jnp.concatenate([queries[r] for r in order], axis=0)
    zero = jnp.zeros_like(q)
    both = jnp.concatenate([jnp.where(low, q, zero), jnp.where(low, zero, q)], axis=1)
    across = jnp.zeros((span, rows), F32)
    for p, r in enumerate(order):
        across = jnp.where(lane == p, matmul_t(side_by_side(keys[r]), both), across)
    length = jnp.concatenate([jnp.full((heads, 1), plan[LENGTH + r]) for r in order], axis=0)
    where = depth * span + lax.broadcasted_iota(jnp.int32, (rows, span), 1)
    allowed = where < length
    s = jnp.where(allowed, across.T * scale, MASKED)

    def per_head(ref):
        pairs = [ref[r].astype(F32) for r in order]
        return jnp.concatenate([jnp.where(low8, x[0:1], x[1:2]) for x in pairs], axis=0)

    fresh = jnp.sum(q.astype(F32) * per_head(new_keys), axis=-1, keepdims=True) * scale
    n = jnp.where(depth == 0, fresh, MASKED)
    level = jnp.floor(jnp.maximum(jnp.max(s, axis=-1, keepdims=True), n))
    w = jnp.where(allowed, jnp.exp2(s - level), 0.0).astype(BF16)
    nw = jnp.where(depth == 0, jnp.exp2(n - level), 0.0).astype(BF16).astype(F32)
    total = jnp.sum(w.astype(F32), axis=-1, keepdims=True) + nw
    added = nw * per_head(new_values)
    column = lax.broadcasted_iota(jnp.int32, (rows, 128), 1)
    stats = jnp.where(column < 64, level, total)
    for p, r in enumerate(order):
        at = slice(p * heads, (p + 1) * heads)
        o = matmul(w[at], side_by_side(values[r]))
        out = own if p < half else other
        out[p % half, 0:8, :] = jnp.where(low8, o[:, 0:width], o[:, width : 2 * width]) + added[at]
        out[p % half, 8:16, :] = stats[at]


def image_kernel(after, arrived, keys, values, out):
    del after
    groups = arrived.shape[0]
    rows = groups * 8
    images, _, patches, width = keys.shape
    scale = 1.0 / (math.sqrt(width) * math.log(2.0))
    q = arrived[:, 0:8, :].reshape(rows, width)
    code = arrived[:, 8:16, :].reshape(rows, width).astype(F32)
    within = jnp.floor(code * 0.5)
    within_lane = within.T[0:1, :]
    low = lax.broadcasted_iota(jnp.int32, (rows, 1), 0) % 8 < 4
    zero = jnp.zeros_like(q)
    both = jnp.concatenate([jnp.where(low, q, zero), jnp.where(low, zero, q)], axis=1)
    across = jnp.zeros((patches, rows), F32)
    for i in range(images):
        across = jnp.where(
            within_lane == float(i), matmul_t(side_by_side(keys[i]), both), across
        )
    s = across.T * scale
    level = jnp.floor(jnp.max(s, axis=-1, keepdims=True))
    w = jnp.exp2(s - level).astype(BF16)
    present = within[:, 0:1] >= 0.0
    total = jnp.where(present, jnp.sum(w.astype(F32), axis=-1, keepdims=True), 0.0)
    nothing = jnp.zeros_like(w)
    o = jnp.zeros((rows, 2 * width), F32)
    for i in range(images):
        o = o + matmul(jnp.where(within[:, 0:1] == float(i), w, nothing), side_by_side(values[i]))
    o = jnp.where(low, o[:, 0:width], o[:, width : 2 * width])
    o = o / jnp.where(present, total, 1.0)
    lane = lax.broadcasted_iota(jnp.int32, (rows, width), 1)
    level_high = level.astype(BF16).astype(F32)
    total_high = total.astype(BF16).astype(F32)
    stats = jnp.where(
        lane < 64,
        jnp.where(lane < 32, level_high, level - level_high),
        jnp.where(lane < 96, total_high, total - total_high),
    )
    second = code - 2.0 * within
    o3 = o.astype(BF16).reshape(groups, 8, width)
    for h in range(2):
        out[:, h, 0:8, :] = o3
        out[:, h, 8:16, :] = (
            jnp.where(second == float(h), stats, 0.0).astype(BF16).reshape(groups, 8, width)
        )


def merge_kernel(plan, back, own, other, states, weight, out, mine, sent, joined):
    half, heads, width = out.shape
    rows = half * heads
    parts = []
    for ref in (own, other):
        stats = ref[:, 8:16, :].reshape(rows, 128)
        parts.append((stats[:, 0:1], stats[:, 64:65], ref[:, 0:8, :].reshape(rows, width)))
    lane = lax.broadcasted_iota(jnp.int32, (heads, 128), 1)
    dead = jnp.where(lane < 32, MASKED, 0.0)
    for k in range(2):
        stats, values = [], []
        for j in range(half):
            source = plan[SOURCE + 2 * (plan[OWN_DEPTH] * half + j) + k]
            at = jnp.maximum(source, 0)
            stats.append(jnp.where(source >= 0, back[at, 8:16, :].astype(F32), dead))
            values.append(back[at, 0:8, :].astype(F32))
        stats = jnp.concatenate(stats, axis=0)
        total = stats[:, 64:65] + stats[:, 96:97]
        parts.append(
            (stats[:, 0:1] + stats[:, 32:33], total, jnp.concatenate(values, axis=0) * total)
        )
    top = functools.reduce(jnp.maximum, [p[0] for p in parts])
    factors = [jnp.exp2(p[0] - top) for p in parts]
    total = sum(f * p[1] for f, p in zip(factors, parts))
    weighted = sum(f * p[2] for f, p in zip(factors, parts))
    value = weighted / total
    out[...] = value.astype(BF16).reshape(out.shape)
    joined[...] = value
    flat = jnp.concatenate(
        [joined[pl.ds(h, half, stride=heads), :] for h in range(heads)], axis=1
    ).astype(BF16)
    row = lax.broadcasted_iota(jnp.int32, (half, 1), 0) - 2 * plan[OWN_MP]
    step = 512
    for c in range(mine.shape[1] // step):
        at = slice(c * step, (c + 1) * step)
        before = jnp.where(row == 1, states[1:2, at], states[0:1, at]).astype(F32)
        before = jnp.where((row == 0) | (row == 1), before, 0.0)
        value = before + matmul(flat, weight[:, at])
        mine[:, at] = value
        sent[:, at] = value.astype(BF16)


def norm_kernel(plan, mine, first, second, third, gain, rest, out):
    x = mine[...] + first[...].astype(F32) + second[...].astype(F32) + third[...].astype(F32)
    kept = x[0:2]
    for c in range(1, x.shape[0] // 2):
        kept = jnp.where(plan[OWN_MP] == c, x[2 * c : 2 * c + 2], kept)
    rest[...] = kept
    spread = jnp.mean(x * x, axis=-1, keepdims=True)
    normed = (x * lax.rsqrt(spread + NORM_EPSILON) * gain[...]).astype(BF16)
    for g in range(out.shape[0]):
        out[g] = normed


def feed_kernel(x, gate, up, down, out, lined):
    a = matmul_t(gate[...], x[...])
    b = matmul_t(up[...], x[...])
    hidden = (a / (1.0 + jnp.exp(-a)) * b).T.astype(BF16)
    tokens = hidden.shape[0]
    tiles = lined.shape[0]
    for q in range(4):
        at = slice(q * tiles * 128, (q + 1) * tiles * 128)
        part = matmul(hidden, down[:, at])
        for c in range(tiles):
            lined[c, pl.ds(q, tokens, stride=4), :] = part[:, c * 128 : (c + 1) * 128]
    for c in range(tiles):
        block = lined[c].astype(BF16).reshape(out.shape[0], 8, 128)
        out[:, :, c * 128 : (c + 1) * 128] = block


def last_kernel(arrived, residual, out):
    total = arrived[0].astype(F32)
    for k in range(1, arrived.shape[0]):
        total = total + arrived[k].astype(F32)
    quarter = arrived.shape[2]
    for t in range(2):
        for q in range(4):
            at = slice(q * quarter, (q + 1) * quarter)
            row = t * 4 + q
            out[t : t + 1, at] = (residual[t : t + 1, at] + total[row : row + 1]).astype(BF16)


def on_device(
    states,
    queries,
    new_keys,
    new_values,
    text_keys,
    text_values,
    text_length,
    image_keys,
    image_values,
    image_slot,
    block_list,
    block_count,
    image_first,
    image_count,
    out_weight,
    norm_gain,
    gate_weight,
    up_weight,
    down_weight,
):
    groups = lax.axis_size("group")
    depths = lax.axis_size("depth")
    ring = lax.axis_size("mp")
    requests, heads, width = queries.shape
    half = requests // depths
    features = states.shape[1]

    integers = (image_slot, block_list, block_count, image_first, image_count, text_length)
    in_place = [in_hbm(x) for x in (*integers, queries)]
    routed, plan = call(
        route_kernel,
        (
            jax.ShapeDtypeStruct((groups, 16, width), BF16),
            jax.ShapeDtypeStruct((SOURCE + 2 * requests,), jnp.int32),
        ),
        [HBM] * 7,
        20_000_000_000,
        100_000,
        "route",
        scratch=[pltpu.SMEM(i.shape, jnp.int32) for i in integers]
        + [pltpu.VMEM(queries.shape, BF16), pltpu.SemaphoreType.DMA((len(in_place),))],
        out_specs=(VMEM, SMEM),
    )(*in_place)
    arrived = lax.all_to_all(routed, "group", 0, 0, tiled=True)
    arrived, plan = lax.optimization_barrier((arrived, plan))

    part = jax.ShapeDtypeStruct((half, 16, width), F32)
    own, other = call(
        text_kernel,
        (part, part),
        [SMEM] + [VMEM] * 5,
        200_000_000,
        4_400_000,
        "text",
    )(plan, queries, new_keys, new_values, text_keys, text_values)
    other = lax.ppermute(other, "depth", [(0, 1), (1, 0)])

    back = call(
        image_kernel,
        jax.ShapeDtypeStruct((groups, depths, 16, width), BF16),
        [VMEM] * 4,
        10_000_000_000,
        5_000_000,
        "image",
    )(own, arrived, image_keys, image_values)
    back, other = lax.optimization_barrier((back, other))
    back = lax.all_to_all(
        back.reshape(groups * depths, 16, width), ("group", "depth"), 0, 0, tiled=True
    )
    attention, mine, sent = call(
        merge_kernel,
        (
            jax.ShapeDtypeStruct((half, heads, width), BF16),
            jax.ShapeDtypeStruct((half, features), F32),
            jax.ShapeDtypeStruct((half, features), BF16),
        ),
        [SMEM] + [VMEM] * 5,
        100_000_000,
        8_800_000,
        "merge",
        scratch=[pltpu.VMEM((half * heads, width), F32)],
    )(plan, back, own, other, states, out_weight)
    passed = [
        lax.ppermute(sent, "mp", [(i, i ^ k) for i in range(ring)]) for k in (1, 3, 2)
    ]
    rest, normed = call(
        norm_kernel,
        (
            jax.ShapeDtypeStruct((2, features), F32),
            jax.ShapeDtypeStruct((groups, half, features), BF16),
        ),
        [SMEM] + [VMEM] * 5,
        10_000_000_000,
        1_600_000,
        "norm",
    )(plan, mine, *passed, norm_gain.reshape(1, features))
    tokens = lax.all_to_all(normed, "group", 0, 0, tiled=True).reshape(groups * half, features)
    peers = groups * ring
    down = call(
        feed_kernel,
        jax.ShapeDtypeStruct((peers, 8, features // 4), BF16),
        [VMEM] * 4,
        1_400_000_000,
        7_000_000,
        "feed",
        scratch=[pltpu.VMEM((features // 512, groups * half * 4, 128), F32)],
    )(tokens, gate_weight.T, up_weight.T, down_weight)
    gathered = lax.all_to_all(down, ("group", "mp"), 0, 0, tiled=True)
    layer_out = call(
        last_kernel,
        jax.ShapeDtypeStruct((2, features), BF16),
        [VMEM] * 2,
        0,
        1_300_000,
        "last",
    )(gathered, rest)
    return attention, layer_out


def solution(mesh):
    placed = (
        P(("group", "depth", "mp"), None),
        P("group", "mp", None),
        P("group", "mp", None),
        P("group", "mp", None),
        P("group", "mp", "depth", None),
        P("group", "mp", "depth", None),
        P("group"),
        P("group", "mp", None, None),
        P("group", "mp", None, None),
        P(),
        P(),
        P(),
        P("group"),
        P("group"),
        P("mp", None),
        P(),
        P(None, ("group", "mp")),
        P(None, ("group", "mp")),
        P(("group", "mp"), None),
    )
    return jax.shard_map(
        on_device,
        mesh=mesh,
        in_specs=placed,
        out_specs=(P(("group", "depth"), "mp", None), P(("group", "depth", "mp"), None)),
        check_vma=False,
    )
```

```python
import functools
import math

import jax
import jax.numpy as jnp
from jax import lax
from jax.experimental import pallas as pl
from jax.experimental.pallas import tpu as pltpu
from jax.sharding import PartitionSpec as P

MASKED = -1e30
NORM_EPSILON = 1e-05
BF16 = jnp.bfloat16
F32 = jnp.float32
VMEM = pl.BlockSpec(memory_space=pltpu.VMEM)
SMEM = pl.BlockSpec(memory_space=pltpu.SMEM)


HBM = pl.BlockSpec(memory_space=pltpu.MemorySpace.HBM)


def call(kernel, out_shape, in_specs, flops, nbytes, name, scratch=(), vmem=16 << 20, out_specs=None):
    return pl.pallas_call(
        kernel,
        out_shape=out_shape,
        in_specs=in_specs,
        out_specs=out_specs or jax.tree.map(lambda _: VMEM, out_shape),
        scratch_shapes=list(scratch),
        cost_estimate=pl.CostEstimate(flops=flops, bytes_accessed=nbytes, transcendentals=0),
        compiler_params=pltpu.CompilerParams(vmem_limit_bytes=vmem),
        name=name,
    )


def in_hbm(x):
    return pltpu.with_memory_space_constraint(x, pltpu.MemorySpace.HBM)


def matmul(a, b):
    return lax.dot_general(a, b, (((1,), (0,)), ((), ())), preferred_element_type=F32)


def matmul_t(a, b):
    return lax.dot_general(a, b, (((1,), (1,)), ((), ())), preferred_element_type=F32)


OWN_DEPTH, OWN_MP, LENGTH, SOURCE = 0, 1, 8, 24


def route_kernel(
    slots_hbm, blocks_hbm, count_hbm, first_hbm, images_hbm, lengths_hbm, queries_hbm, out, plan, *scratch
):
    slots, blocks, count, first, images, lengths, queries, sems = scratch
    copies = [
        pltpu.make_async_copy(src, dst, sems.at[k])
        for k, (src, dst) in enumerate(
            (
                (first_hbm, first),
                (images_hbm, images),
                (count_hbm, count),
                (blocks_hbm, blocks),
                (slots_hbm, slots),
                (lengths_hbm, lengths),
                (queries_hbm, queries),
            )
        )
    ]
    for copy in copies:
        copy.start()
    group, depth = lax.axis_index("group"), lax.axis_index("depth")
    requests = queries.shape[0]
    half = requests // 2
    out[...] = jnp.full(out.shape, -1.0, BF16)
    plan[OWN_DEPTH] = depth
    plan[OWN_MP] = lax.axis_index("mp")
    for copy in copies:
        copy.wait()
    listed = count[group]

    def source(place):
        slot = slots[blocks[group, jnp.minimum(place, blocks.shape[1] - 1)]]
        return slot >> 3, slot & 7

    for r in range(requests):
        start, read = first[r], images[r]
        plan[LENGTH + r] = lengths[r]
        for k in range(2):
            place = start + k
            owner, within = source(place)
            live = (k < read) & (place < listed)
            plan[SOURCE + 2 * r + k] = jnp.where(live, owner * 2 + (place & 1), -1)

            @pl.when(live & ((place & 1) == depth))
            def _():
                out[owner, 0:8, :] = queries[r]
                code = (within * 2 + r // half).astype(F32)
                out[owner, 8:16, :] = jnp.full((8, 128), code, F32).astype(BF16)


def side_by_side(pair):
    return jnp.concatenate([pair[0], pair[1]], axis=1)


def text_kernel(plan, queries, new_keys, new_values, keys, values, own, other):
    depth = plan[OWN_DEPTH]
    requests, heads, width = queries.shape
    half = requests // 2
    rows = requests * heads
    span = keys.shape[2]
    scale = 1.0 / (math.sqrt(width) * math.log(2.0))
    order = [(p + half * depth) % requests for p in range(requests)]
    low8 = lax.broadcasted_iota(jnp.int32, (heads, 1), 0) < heads // 2
    low = lax.broadcasted_iota(jnp.int32, (rows, 1), 0) % heads < heads // 2
    lane = lax.broadcasted_iota(jnp.int32, (1, rows), 1) // heads
    q = jnp.concatenate([queries[r] for r in order], axis=0)
    zero = jnp.zeros_like(q)
    both = jnp.concatenate([jnp.where(low, q, zero), jnp.where(low, zero, q)], axis=1)
    across = jnp.zeros((span, rows), F32)
    for p, r in enumerate(order):
        across = jnp.where(lane == p, matmul_t(side_by_side(keys[r]), both), across)
    length = jnp.concatenate([jnp.full((heads, 1), plan[LENGTH + r]) for r in order], axis=0)
    where = depth * span + lax.broadcasted_iota(jnp.int32, (rows, span), 1)
    allowed = where < length
    s = jnp.where(allowed, across.T * scale, MASKED)

    def per_head(ref):
        pairs = [ref[r].astype(F32) for r in order]
        return jnp.concatenate([jnp.where(low8, x[0:1], x[1:2]) for x in pairs], axis=0)

    fresh = jnp.sum(q.astype(F32) * per_head(new_keys), axis=-1, keepdims=True) * scale
    n = jnp.where(depth == 0, fresh, MASKED)
    level = jnp.floor(jnp.maximum(jnp.max(s, axis=-1, keepdims=True), n))
    w = jnp.where(allowed, jnp.exp2(s - level), 0.0).astype(BF16)
    nw = jnp.where(depth == 0, jnp.exp2(n - level), 0.0).astype(BF16).astype(F32)
    total = jnp.sum(w.astype(F32), axis=-1, keepdims=True) + nw
    added = nw * per_head(new_values)
    column = lax.broadcasted_iota(jnp.int32, (rows, 128), 1)
    stats = jnp.where(column < 64, level, total)
    for p, r in enumerate(order):
        at = slice(p * heads, (p + 1) * heads)
        o = matmul(w[at], side_by_side(values[r]))
        out = own if p < half else other
        out[p % half, 0:8, :] = jnp.where(low8, o[:, 0:width], o[:, width : 2 * width]) + added[at]
        out[p % half, 8:16, :] = stats[at]


def image_kernel(after, arrived, keys, values, out):
    del after
    groups = arrived.shape[0]
    rows = groups * 8
    images, _, patches, width = keys.shape
    scale = 1.0 / (math.sqrt(width) * math.log(2.0))
    q = arrived[:, 0:8, :].reshape(rows, width)
    code = arrived[:, 8:16, :].reshape(rows, width).astype(F32)
    within = jnp.floor(code * 0.5)
    within_lane = within.T[0:1, :]
    low = lax.broadcasted_iota(jnp.int32, (rows, 1), 0) % 8 < 4
    zero = jnp.zeros_like(q)
    both = jnp.concatenate([jnp.where(low, q, zero), jnp.where(low, zero, q)], axis=1)
    across = jnp.zeros((patches, rows), F32)
    for i in range(images):
        across = jnp.where(
            within_lane == float(i), matmul_t(side_by_side(keys[i]), both), across
        )
    s = across.T * scale
    level = jnp.floor(jnp.max(s, axis=-1, keepdims=True))
    w = jnp.exp2(s - level).astype(BF16)
    present = within[:, 0:1] >= 0.0
    total = jnp.where(present, jnp.sum(w.astype(F32), axis=-1, keepdims=True), 0.0)
    nothing = jnp.zeros_like(w)
    o = jnp.zeros((rows, 2 * width), F32)
    for i in range(images):
        o = o + matmul(jnp.where(within[:, 0:1] == float(i), w, nothing), side_by_side(values[i]))
    o = jnp.where(low, o[:, 0:width], o[:, width : 2 * width])
    o = o / jnp.where(present, total, 1.0)
    lane = lax.broadcasted_iota(jnp.int32, (rows, width), 1)
    level_high = level.astype(BF16).astype(F32)
    total_high = total.astype(BF16).astype(F32)
    stats = jnp.where(
        lane < 64,
        jnp.where(lane < 32, level_high, level - level_high),
        jnp.where(lane < 96, total_high, total - total_high),
    )
    second = code - 2.0 * within
    o3 = o.astype(BF16).reshape(groups, 8, width)
    for h in range(2):
        out[:, h, 0:8, :] = o3
        out[:, h, 8:16, :] = (
            jnp.where(second == float(h), stats, 0.0).astype(BF16).reshape(groups, 8, width)
        )


def merge_kernel(plan, back, own, other, states, weight, out, mine, sent, joined):
    half, heads, width = out.shape
    rows = half * heads
    parts = []
    for ref in (own, other):
        stats = ref[:, 8:16, :].reshape(rows, 128)
        parts.append((stats[:, 0:1], stats[:, 64:65], ref[:, 0:8, :].reshape(rows, width)))
    lane = lax.broadcasted_iota(jnp.int32, (heads, 128), 1)
    dead = jnp.where(lane < 32, MASKED, 0.0)
    for k in range(2):
        stats, values = [], []
        for j in range(half):
            source = plan[SOURCE + 2 * (plan[OWN_DEPTH] * half + j) + k]
            at = jnp.maximum(source, 0)
            stats.append(jnp.where(source >= 0, back[at, 8:16, :].astype(F32), dead))
            values.append(back[at, 0:8, :].astype(F32))
        stats = jnp.concatenate(stats, axis=0)
        total = stats[:, 64:65] + stats[:, 96:97]
        parts.append(
            (stats[:, 0:1] + stats[:, 32:33], total, jnp.concatenate(values, axis=0) * total)
        )
    top = functools.reduce(jnp.maximum, [p[0] for p in parts])
    factors = [jnp.exp2(p[0] - top) for p in parts]
    total = sum(f * p[1] for f, p in zip(factors, parts))
    weighted = sum(f * p[2] for f, p in zip(factors, parts))
    value = weighted / total
    out[...] = value.astype(BF16).reshape(out.shape)
    joined[...] = value
    flat = jnp.concatenate(
        [joined[pl.ds(h, half, stride=heads), :] for h in range(heads)], axis=1
    ).astype(BF16)
    row = lax.broadcasted_iota(jnp.int32, (half, 1), 0) - 2 * plan[OWN_MP]
    step = 512
    for c in range(mine.shape[1] // step):
        at = slice(c * step, (c + 1) * step)
        before = jnp.where(row == 1, states[1:2, at], states[0:1, at]).astype(F32)
        before = jnp.where((row == 0) | (row == 1), before, 0.0)
        value = before + matmul(flat, weight[:, at])
        mine[:, at] = value
        sent[:, at] = value.astype(BF16)


def norm_kernel(plan, mine, first, second, third, gain, rest, out):
    x = mine[...] + first[...].astype(F32) + second[...].astype(F32) + third[...].astype(F32)
    kept = x[0:2]
    for c in range(1, x.shape[0] // 2):
        kept = jnp.where(plan[OWN_MP] == c, x[2 * c : 2 * c + 2], kept)
    rest[...] = kept
    spread = jnp.mean(x * x, axis=-1, keepdims=True)
    normed = (x * lax.rsqrt(spread + NORM_EPSILON) * gain[...]).astype(BF16)
    for g in range(out.shape[0]):
        out[g] = normed


def feed_kernel(x, gate, up, down, out, lined):
    a = matmul_t(gate[...], x[...])
    b = matmul_t(up[...], x[...])
    hidden = (a / (1.0 + jnp.exp(-a)) * b).T.astype(BF16)
    tokens = hidden.shape[0]
    tiles = lined.shape[0]
    for q in range(4):
        at = slice(q * tiles * 128, (q + 1) * tiles * 128)
        part = matmul(hidden, down[:, at])
        for c in range(tiles):
            lined[c, pl.ds(q, tokens, stride=4), :] = part[:, c * 128 : (c + 1) * 128]
    for c in range(tiles):
        block = lined[c].astype(BF16).reshape(out.shape[0], 8, 128)
        out[:, :, c * 128 : (c + 1) * 128] = block


def last_kernel(arrived, residual, out):
    total = arrived[0].astype(F32)
    for k in range(1, arrived.shape[0]):
        total = total + arrived[k].astype(F32)
    quarter = arrived.shape[2]
    for t in range(2):
        for q in range(4):
            at = slice(q * quarter, (q + 1) * quarter)
            row = t * 4 + q
            out[t : t + 1, at] = (residual[t : t + 1, at] + total[row : row + 1]).astype(BF16)


def on_device(
    states,
    queries,
    new_keys,
    new_values,
    text_keys,
    text_values,
    text_length,
    image_keys,
    image_values,
    image_slot,
    block_list,
    block_count,
    image_first,
    image_count,
    out_weight,
    norm_gain,
    gate_weight,
    up_weight,
    down_weight,
):
    groups = lax.axis_size("group")
    depths = lax.axis_size("depth")
    ring = lax.axis_size("mp")
    requests, heads, width = queries.shape
    half = requests // depths
    features = states.shape[1]

    integers = (image_slot, block_list, block_count, image_first, image_count, text_length)
    in_place = [in_hbm(x) for x in (*integers, queries)]
    routed, plan = call(
        route_kernel,
        (
            jax.ShapeDtypeStruct((groups, 16, width), BF16),
            jax.ShapeDtypeStruct((SOURCE + 2 * requests,), jnp.int32),
        ),
        [HBM] * 7,
        20_000_000_000,
        100_000,
        "route",
        scratch=[pltpu.SMEM(i.shape, jnp.int32) for i in integers]
        + [pltpu.VMEM(queries.shape, BF16), pltpu.SemaphoreType.DMA((len(in_place),))],
        out_specs=(VMEM, SMEM),
    )(*in_place)
    arrived = lax.all_to_all(routed, "group", 0, 0, tiled=True)
    arrived, plan = lax.optimization_barrier((arrived, plan))

    part = jax.ShapeDtypeStruct((half, 16, width), F32)
    own, other = call(
        text_kernel,
        (part, part),
        [SMEM] + [VMEM] * 5,
        200_000_000,
        4_400_000,
        "text",
    )(plan, queries, new_keys, new_values, text_keys, text_values)
    other = lax.ppermute(other, "depth", [(0, 1), (1, 0)])

    back = call(
        image_kernel,
        jax.ShapeDtypeStruct((groups, depths, 16, width), BF16),
        [VMEM] * 4,
        10_000_000_000,
        5_000_000,
        "image",
    )(own, arrived, image_keys, image_values)
    back, other = lax.optimization_barrier((back, other))
    back = lax.all_to_all(
        back.reshape(groups * depths, 16, width), ("group", "depth"), 0, 0, tiled=True
    )
    attention, mine, sent = call(
        merge_kernel,
        (
            jax.ShapeDtypeStruct((half, heads, width), BF16),
            jax.ShapeDtypeStruct((half, features), F32),
            jax.ShapeDtypeStruct((half, features), BF16),
        ),
        [SMEM] + [VMEM] * 5,
        100_000_000,
        8_800_000,
        "merge",
        scratch=[pltpu.VMEM((half * heads, width), F32)],
    )(plan, back, own, other, states, out_weight)
    passed = [
        lax.ppermute(sent, "mp", [(i, i ^ k) for i in range(ring)]) for k in (2, 3, 1)
    ]
    rest, normed = call(
        norm_kernel,
        (
            jax.ShapeDtypeStruct((2, features), F32),
            jax.ShapeDtypeStruct((groups, half, features), BF16),
        ),
        [SMEM] + [VMEM] * 5,
        10_000_000_000,
        1_600_000,
        "norm",
    )(plan, mine, *passed, norm_gain.reshape(1, features))
    tokens = lax.all_to_all(normed, "group", 0, 0, tiled=True).reshape(groups * half, features)
    peers = groups * ring
    down = call(
        feed_kernel,
        jax.ShapeDtypeStruct((peers, 8, features // 4), BF16),
        [VMEM] * 4,
        1_400_000_000,
        7_000_000,
        "feed",
        scratch=[pltpu.VMEM((features // 512, groups * half * 4, 128), F32)],
    )(tokens, gate_weight.T, up_weight.T, down_weight)
    gathered = lax.all_to_all(down, ("group", "mp"), 0, 0, tiled=True)
    layer_out = call(
        last_kernel,
        jax.ShapeDtypeStruct((2, features), BF16),
        [VMEM] * 2,
        0,
        1_300_000,
        "last",
    )(gathered, rest)
    return attention, layer_out


def solution(mesh):
    placed = (
        P(("group", "depth", "mp"), None),
        P("group", "mp", None),
        P("group", "mp", None),
        P("group", "mp", None),
        P("group", "mp", "depth", None),
        P("group", "mp", "depth", None),
        P("group"),
        P("group", "mp", None, None),
        P("group", "mp", None, None),
        P(),
        P(),
        P(),
        P("group"),
        P("group"),
        P("mp", None),
        P(),
        P(None, ("group", "mp")),
        P(None, ("group", "mp")),
        P(("group", "mp"), None),
    )
    return jax.shard_map(
        on_device,
        mesh=mesh,
        in_specs=placed,
        out_specs=(P(("group", "depth"), "mp", None), P(("group", "depth", "mp"), None)),
        check_vma=False,
    )
```

```python
import functools
import math

import jax
import jax.numpy as jnp
from jax import lax
from jax.experimental import pallas as pl
from jax.experimental.pallas import tpu as pltpu
from jax.sharding import PartitionSpec as P

MASKED = -1e30
NORM_EPSILON = 1e-05
BF16 = jnp.bfloat16
F32 = jnp.float32
VMEM = pl.BlockSpec(memory_space=pltpu.VMEM)
SMEM = pl.BlockSpec(memory_space=pltpu.SMEM)


HBM = pl.BlockSpec(memory_space=pltpu.MemorySpace.HBM)


def call(kernel, out_shape, in_specs, flops, nbytes, name, scratch=(), vmem=16 << 20, out_specs=None):
    return pl.pallas_call(
        kernel,
        out_shape=out_shape,
        in_specs=in_specs,
        out_specs=out_specs or jax.tree.map(lambda _: VMEM, out_shape),
        scratch_shapes=list(scratch),
        cost_estimate=pl.CostEstimate(flops=flops, bytes_accessed=nbytes, transcendentals=0),
        compiler_params=pltpu.CompilerParams(vmem_limit_bytes=vmem),
        name=name,
    )


def in_hbm(x):
    return pltpu.with_memory_space_constraint(x, pltpu.MemorySpace.HBM)


def matmul(a, b):
    return lax.dot_general(a, b, (((1,), (0,)), ((), ())), preferred_element_type=F32)


def matmul_t(a, b):
    return lax.dot_general(a, b, (((1,), (1,)), ((), ())), preferred_element_type=F32)


def route_kernel(
    slots_hbm, blocks_hbm, count_hbm, first_hbm, images_hbm, queries_hbm, out, plan, *scratch
):
    slots, blocks, count, first, images, queries, sems = scratch
    copies = [
        pltpu.make_async_copy(src, dst, sems.at[k])
        for k, (src, dst) in enumerate(
            (
                (first_hbm, first),
                (images_hbm, images),
                (count_hbm, count),
                (blocks_hbm, blocks),
                (slots_hbm, slots),
                (queries_hbm, queries),
            )
        )
    ]
    for copy in copies:
        copy.start()
    group, depth = lax.axis_index("group"), lax.axis_index("depth")
    requests = queries.shape[0]
    half = requests // 2
    out[...] = jnp.full(out.shape, -1.0, BF16)
    for copy in copies:
        copy.wait()
    listed = count[group]

    def source(place):
        slot = slots[blocks[group, jnp.minimum(place, blocks.shape[1] - 1)]]
        return slot >> 3, slot & 7

    for r in range(requests):
        start, read = first[r], images[r]
        for k in range(2):
            place = start + k
            owner, within = source(place)
            live = (k < read) & (place < listed)
            plan[2 * r + k] = jnp.where(live, owner * 2 + (place & 1), -1)

            @pl.when(live & ((place & 1) == depth))
            def _():
                out[owner, 0:8, :] = queries[r]
                code = (within * 2 + r // half).astype(F32)
                out[owner, 8:16, :] = jnp.full((8, 128), code, F32).astype(BF16)


def side_by_side(pair):
    return jnp.concatenate([pair[0], pair[1]], axis=1)


def text_kernel(lengths_hbm, queries, new_keys, new_values, keys, values, own, other, lengths, sem):
    fetch = pltpu.make_async_copy(lengths_hbm, lengths, sem)
    fetch.start()
    depth = lax.axis_index("depth")
    requests, heads, width = queries.shape
    half = requests // 2
    rows = requests * heads
    span = keys.shape[2]
    scale = 1.0 / (math.sqrt(width) * math.log(2.0))
    order = [(p + half * depth) % requests for p in range(requests)]
    low8 = lax.broadcasted_iota(jnp.int32, (heads, 1), 0) < heads // 2
    low = lax.broadcasted_iota(jnp.int32, (rows, 1), 0) % heads < heads // 2
    lane = lax.broadcasted_iota(jnp.int32, (1, rows), 1) // heads
    q = jnp.concatenate([queries[r] for r in order], axis=0)
    zero = jnp.zeros_like(q)
    both = jnp.concatenate([jnp.where(low, q, zero), jnp.where(low, zero, q)], axis=1)
    across = jnp.zeros((span, rows), F32)
    for p, r in enumerate(order):
        across = jnp.where(lane == p, matmul_t(side_by_side(keys[r]), both), across)
    fetch.wait()
    length = jnp.concatenate([jnp.full((heads, 1), lengths[r]) for r in order], axis=0)
    where = depth * span + lax.broadcasted_iota(jnp.int32, (rows, span), 1)
    allowed = where < length
    s = jnp.where(allowed, across.T * scale, MASKED)

    def per_head(ref):
        pairs = [ref[r].astype(F32) for r in order]
        return jnp.concatenate([jnp.where(low8, x[0:1], x[1:2]) for x in pairs], axis=0)

    fresh = jnp.sum(q.astype(F32) * per_head(new_keys), axis=-1, keepdims=True) * scale
    n = jnp.where(depth == 0, fresh, MASKED)
    level = jnp.floor(jnp.maximum(jnp.max(s, axis=-1, keepdims=True), n))
    w = jnp.where(allowed, jnp.exp2(s - level), 0.0).astype(BF16)
    nw = jnp.where(depth == 0, jnp.exp2(n - level), 0.0).astype(BF16).astype(F32)
    total = jnp.sum(w.astype(F32), axis=-1, keepdims=True) + nw
    added = nw * per_head(new_values)
    column = lax.broadcasted_iota(jnp.int32, (rows, 128), 1)
    stats = jnp.where(column < 64, level, total)
    for p, r in enumerate(order):
        at = slice(p * heads, (p + 1) * heads)
        o = matmul(w[at], side_by_side(values[r]))
        out = own if p < half else other
        out[p % half, 0:8, :] = jnp.where(low8, o[:, 0:width], o[:, width : 2 * width]) + added[at]
        out[p % half, 8:16, :] = stats[at]


def image_kernel(after, arrived, keys, values, out):
    del after
    groups = arrived.shape[0]
    rows = groups * 8
    images, _, patches, width = keys.shape
    scale = 1.0 / (math.sqrt(width) * math.log(2.0))
    q = arrived[:, 0:8, :].reshape(rows, width)
    code = arrived[:, 8:16, :].reshape(rows, width).astype(F32)
    within = jnp.floor(code * 0.5)
    within_lane = within.T[0:1, :]
    low = lax.broadcasted_iota(jnp.int32, (rows, 1), 0) % 8 < 4
    zero = jnp.zeros_like(q)
    both = jnp.concatenate([jnp.where(low, q, zero), jnp.where(low, zero, q)], axis=1)
    across = jnp.zeros((patches, rows), F32)
    for i in range(images):
        across = jnp.where(
            within_lane == float(i), matmul_t(side_by_side(keys[i]), both), across
        )
    s = across.T * scale
    level = jnp.floor(jnp.max(s, axis=-1, keepdims=True))
    w = jnp.exp2(s - level).astype(BF16)
    present = within[:, 0:1] >= 0.0
    total = jnp.where(present, jnp.sum(w.astype(F32), axis=-1, keepdims=True), 0.0)
    nothing = jnp.zeros_like(w)
    o = jnp.zeros((rows, 2 * width), F32)
    for i in range(images):
        o = o + matmul(jnp.where(within[:, 0:1] == float(i), w, nothing), side_by_side(values[i]))
    o = jnp.where(low, o[:, 0:width], o[:, width : 2 * width])
    o = o / jnp.where(present, total, 1.0)
    lane = lax.broadcasted_iota(jnp.int32, (rows, width), 1)
    level_high = level.astype(BF16).astype(F32)
    total_high = total.astype(BF16).astype(F32)
    stats = jnp.where(
        lane < 64,
        jnp.where(lane < 32, level_high, level - level_high),
        jnp.where(lane < 96, total_high, total - total_high),
    )
    second = code - 2.0 * within
    o3 = o.astype(BF16).reshape(groups, 8, width)
    for h in range(2):
        out[:, h, 0:8, :] = o3
        out[:, h, 8:16, :] = (
            jnp.where(second == float(h), stats, 0.0).astype(BF16).reshape(groups, 8, width)
        )


def merge_kernel(plan, back, own, other, states, weight, out, mine, sent, joined, sources, value16, sems):
    fetch = pltpu.make_async_copy(plan, sources, sems.at[0])
    fetch.start()
    half, heads, width = out.shape
    rows = half * heads
    parts = []
    for ref in (own, other):
        stats = ref[:, 8:16, :].reshape(rows, 128)
        parts.append((stats[:, 0:1], stats[:, 64:65], ref[:, 0:8, :].reshape(rows, width)))
    lane = lax.broadcasted_iota(jnp.int32, (heads, 128), 1)
    dead = jnp.where(lane < 32, MASKED, 0.0)
    begin = 2 * half * lax.axis_index("depth")
    fetch.wait()
    for k in range(2):
        stats, values = [], []
        for j in range(half):
            source = sources[begin + 2 * j + k]
            at = jnp.maximum(source, 0)
            stats.append(jnp.where(source >= 0, back[at, 8:16, :].astype(F32), dead))
            values.append(back[at, 0:8, :].astype(F32))
        stats = jnp.concatenate(stats, axis=0)
        total = stats[:, 64:65] + stats[:, 96:97]
        parts.append(
            (stats[:, 0:1] + stats[:, 32:33], total, jnp.concatenate(values, axis=0) * total)
        )
    top = functools.reduce(jnp.maximum, [p[0] for p in parts])
    factors = [jnp.exp2(p[0] - top) for p in parts]
    total = sum(f * p[1] for f, p in zip(factors, parts))
    weighted = sum(f * p[2] for f, p in zip(factors, parts))
    value = weighted / total
    joined[...] = value
    value16[...] = value.astype(BF16).reshape(out.shape)
    leave = pltpu.make_async_copy(value16, out, sems.at[1])
    leave.start()
    flat = jnp.concatenate(
        [joined[pl.ds(h, half, stride=heads), :] for h in range(heads)], axis=1
    ).astype(BF16)
    row = lax.broadcasted_iota(jnp.int32, (half, 1), 0) - 2 * lax.axis_index("mp")
    step = 512
    for c in range(mine.shape[1] // step):
        at = slice(c * step, (c + 1) * step)
        before = jnp.where(row == 1, states[1:2, at], states[0:1, at]).astype(F32)
        before = jnp.where((row == 0) | (row == 1), before, 0.0)
        value = before + matmul(flat, weight[:, at])
        mine[:, at] = value
        sent[:, at] = value.astype(BF16)
    leave.wait()


def norm_kernel(mine, first, second, third, gain, rest, out):
    x = mine[...] + first[...].astype(F32) + second[...].astype(F32) + third[...].astype(F32)
    position = lax.axis_index("mp")
    kept = x[0:2]
    for c in range(1, x.shape[0] // 2):
        kept = jnp.where(position == c, x[2 * c : 2 * c + 2], kept)
    rest[...] = kept
    spread = jnp.mean(x * x, axis=-1, keepdims=True)
    normed = (x * lax.rsqrt(spread + NORM_EPSILON) * gain[...]).astype(BF16)
    for g in range(out.shape[0]):
        out[g] = normed


def feed_kernel(x, gate, up, down, out, lined):
    a = matmul_t(gate[...], x[...])
    b = matmul_t(up[...], x[...])
    hidden = (a / (1.0 + jnp.exp(-a)) * b).T.astype(BF16)
    tokens = hidden.shape[0]
    tiles = lined.shape[0]
    for q in range(4):
        at = slice(q * tiles * 128, (q + 1) * tiles * 128)
        part = matmul(hidden, down[:, at])
        for c in range(tiles):
            lined[c, pl.ds(q, tokens, stride=4), :] = part[:, c * 128 : (c + 1) * 128]
    for c in range(tiles):
        block = lined[c].astype(BF16).reshape(out.shape[0], 8, 128)
        out[:, :, c * 128 : (c + 1) * 128] = block


def last_kernel(arrived, residual, out):
    total = arrived[0].astype(F32)
    for k in range(1, arrived.shape[0]):
        total = total + arrived[k].astype(F32)
    quarter = arrived.shape[2]
    for t in range(2):
        for q in range(4):
            at = slice(q * quarter, (q + 1) * quarter)
            row = t * 4 + q
            out[t : t + 1, at] = (residual[t : t + 1, at] + total[row : row + 1]).astype(BF16)


def on_device(
    states,
    queries,
    new_keys,
    new_values,
    text_keys,
    text_values,
    text_length,
    image_keys,
    image_values,
    image_slot,
    block_list,
    block_count,
    image_first,
    image_count,
    out_weight,
    norm_gain,
    gate_weight,
    up_weight,
    down_weight,
):
    groups = lax.axis_size("group")
    depths = lax.axis_size("depth")
    ring = lax.axis_size("mp")
    requests, heads, width = queries.shape
    half = requests // depths
    features = states.shape[1]

    integers = (image_slot, block_list, block_count, image_first, image_count)
    in_place = [in_hbm(x) for x in (*integers, queries)]
    routed, plan = call(
        route_kernel,
        (
            jax.ShapeDtypeStruct((groups, 16, width), BF16),
            jax.ShapeDtypeStruct((2 * requests,), jnp.int32),
        ),
        [HBM] * 6,
        20_000_000_000,
        100_000,
        "route",
        scratch=[pltpu.SMEM(i.shape, jnp.int32) for i in integers]
        + [pltpu.VMEM(queries.shape, BF16), pltpu.SemaphoreType.DMA((len(in_place),))],
        out_specs=(VMEM, SMEM),
    )(*in_place)
    arrived = lax.all_to_all(routed, "group", 0, 0, tiled=True)
    arrived, queries = lax.optimization_barrier((arrived, queries))

    part = jax.ShapeDtypeStruct((half, 16, width), F32)
    own, other = call(
        text_kernel,
        (part, part),
        [HBM] + [VMEM] * 5,
        200_000_000,
        4_400_000,
        "text",
        scratch=[pltpu.SMEM(text_length.shape, jnp.int32), pltpu.SemaphoreType.DMA],
    )(in_hbm(text_length), queries, new_keys, new_values, text_keys, text_values)
    other = lax.ppermute(other, "depth", [(0, 1), (1, 0)])

    back = call(
        image_kernel,
        jax.ShapeDtypeStruct((groups, depths, 16, width), BF16),
        [VMEM] * 4,
        10_000_000_000,
        5_000_000,
        "image",
    )(own, arrived, image_keys, image_values)
    back, other = lax.optimization_barrier((back, other))
    back = lax.all_to_all(
        back.reshape(groups * depths, 16, width), ("group", "depth"), 0, 0, tiled=True
    )
    attention, mine, sent = call(
        merge_kernel,
        (
            jax.ShapeDtypeStruct((half, heads, width), BF16),
            jax.ShapeDtypeStruct((half, features), F32),
            jax.ShapeDtypeStruct((half, features), BF16),
        ),
        [VMEM] * 6,
        100_000_000,
        8_800_000,
        "merge",
        scratch=[
            pltpu.VMEM((half * heads, width), F32),
            pltpu.SMEM(plan.shape, jnp.int32),
            pltpu.VMEM((half, heads, width), BF16),
            pltpu.SemaphoreType.DMA((2,)),
        ],
        out_specs=(HBM, VMEM, VMEM),
    )(plan, back, own, other, states, out_weight)
    passed = [
        lax.ppermute(sent, "mp", [(i, i ^ k) for i in range(ring)]) for k in (2, 3, 1)
    ]
    rest, normed = call(
        norm_kernel,
        (
            jax.ShapeDtypeStruct((2, features), F32),
            jax.ShapeDtypeStruct((groups, half, features), BF16),
        ),
        [VMEM] * 5,
        10_000_000_000,
        1_600_000,
        "norm",
    )(mine, *passed, norm_gain.reshape(1, features))
    tokens = lax.all_to_all(normed, "group", 0, 0, tiled=True).reshape(groups * half, features)
    peers = groups * ring
    down = call(
        feed_kernel,
        jax.ShapeDtypeStruct((peers, 8, features // 4), BF16),
        [VMEM] * 4,
        1_400_000_000,
        7_000_000,
        "feed",
        scratch=[pltpu.VMEM((features // 512, groups * half * 4, 128), F32)],
    )(tokens, gate_weight.T, up_weight.T, down_weight)
    gathered = lax.all_to_all(down, ("group", "mp"), 0, 0, tiled=True)
    layer_out = call(
        last_kernel,
        jax.ShapeDtypeStruct((2, features), BF16),
        [VMEM] * 2,
        0,
        1_300_000,
        "last",
    )(gathered, rest)
    return attention, layer_out


def solution(mesh):
    placed = (
        P(("group", "depth", "mp"), None),
        P("group", "mp", None),
        P("group", "mp", None),
        P("group", "mp", None),
        P("group", "mp", "depth", None),
        P("group", "mp", "depth", None),
        P("group"),
        P("group", "mp", None, None),
        P("group", "mp", None, None),
        P(),
        P(),
        P(),
        P("group"),
        P("group"),
        P("mp", None),
        P(),
        P(None, ("group", "mp")),
        P(None, ("group", "mp")),
        P(("group", "mp"), None),
    )
    return jax.shard_map(
        on_device,
        mesh=mesh,
        in_specs=placed,
        out_specs=(P(("group", "depth"), "mp", None), P(("group", "depth", "mp"), None)),
        check_vma=False,
    )
```

```python
import functools
import math

import jax
import jax.numpy as jnp
from jax import lax
from jax.experimental import pallas as pl
from jax.experimental.pallas import tpu as pltpu
from jax.sharding import PartitionSpec as P

MASKED = -1e30
NORM_EPSILON = 1e-05
BF16 = jnp.bfloat16
F32 = jnp.float32
VMEM = pl.BlockSpec(memory_space=pltpu.VMEM)
SMEM = pl.BlockSpec(memory_space=pltpu.SMEM)


HBM = pl.BlockSpec(memory_space=pltpu.MemorySpace.HBM)


def call(kernel, out_shape, in_specs, flops, nbytes, name, scratch=(), vmem=16 << 20, out_specs=None):
    return pl.pallas_call(
        kernel,
        out_shape=out_shape,
        in_specs=in_specs,
        out_specs=out_specs or jax.tree.map(lambda _: VMEM, out_shape),
        scratch_shapes=list(scratch),
        cost_estimate=pl.CostEstimate(flops=flops, bytes_accessed=nbytes, transcendentals=0),
        compiler_params=pltpu.CompilerParams(vmem_limit_bytes=vmem),
        name=name,
    )


def in_hbm(x):
    return pltpu.with_memory_space_constraint(x, pltpu.MemorySpace.HBM)


def matmul(a, b):
    return lax.dot_general(a, b, (((1,), (0,)), ((), ())), preferred_element_type=F32)


def matmul_t(a, b):
    return lax.dot_general(a, b, (((1,), (1,)), ((), ())), preferred_element_type=F32)


def route_kernel(
    slots_hbm, blocks_hbm, count_hbm, first_hbm, images_hbm, queries_hbm, out, plan, *scratch
):
    slots, blocks, count, first, images, queries, sems = scratch
    copies = [
        pltpu.make_async_copy(src, dst, sems.at[k])
        for k, (src, dst) in enumerate(
            (
                (first_hbm, first),
                (images_hbm, images),
                (count_hbm, count),
                (blocks_hbm, blocks),
                (slots_hbm, slots),
                (queries_hbm, queries),
            )
        )
    ]
    for copy in copies:
        copy.start()
    group, depth = lax.axis_index("group"), lax.axis_index("depth")
    requests = queries.shape[0]
    half = requests // 2
    out[...] = jnp.full(out.shape, -1.0, BF16)
    for copy in copies:
        copy.wait()
    listed = count[group]

    def source(place):
        slot = slots[blocks[group, jnp.minimum(place, blocks.shape[1] - 1)]]
        return slot >> 3, slot & 7

    for r in range(requests):
        start, read = first[r], images[r]
        for k in range(2):
            place = start + k
            owner, within = source(place)
            live = (k < read) & (place < listed)
            sender = jnp.where(live, owner * 2 + (place & 1), -1)
            plan[k, 8 * r : 8 * r + 8, :] = jnp.full((8, 128), sender, jnp.int32)

            @pl.when(live & ((place & 1) == depth))
            def _():
                out[owner, 0:8, :] = queries[r]
                code = (within * 2 + r // half).astype(F32)
                out[owner, 8:16, :] = jnp.full((8, 128), code, F32).astype(BF16)


def side_by_side(pair):
    return jnp.concatenate([pair[0], pair[1]], axis=1)


def text_kernel(lengths_hbm, queries, new_keys, new_values, keys, values, own, other, lengths, sem):
    fetch = pltpu.make_async_copy(lengths_hbm, lengths, sem)
    fetch.start()
    depth = lax.axis_index("depth")
    requests, heads, width = queries.shape
    half = requests // 2
    rows = requests * heads
    span = keys.shape[2]
    scale = 1.0 / (math.sqrt(width) * math.log(2.0))
    order = [(p + half * depth) % requests for p in range(requests)]
    low8 = lax.broadcasted_iota(jnp.int32, (heads, 1), 0) < heads // 2
    low = lax.broadcasted_iota(jnp.int32, (rows, 1), 0) % heads < heads // 2
    lane = lax.broadcasted_iota(jnp.int32, (1, rows), 1) // heads
    q = jnp.concatenate([queries[r] for r in order], axis=0)
    zero = jnp.zeros_like(q)
    both = jnp.concatenate([jnp.where(low, q, zero), jnp.where(low, zero, q)], axis=1)
    across = jnp.zeros((span, rows), F32)
    for p, r in enumerate(order):
        across = jnp.where(lane == p, matmul_t(side_by_side(keys[r]), both), across)
    fetch.wait()
    length = jnp.concatenate([jnp.full((heads, 1), lengths[r]) for r in order], axis=0)
    where = depth * span + lax.broadcasted_iota(jnp.int32, (rows, span), 1)
    allowed = where < length
    s = jnp.where(allowed, across.T * scale, MASKED)

    def per_head(ref):
        pairs = [ref[r].astype(F32) for r in order]
        return jnp.concatenate([jnp.where(low8, x[0:1], x[1:2]) for x in pairs], axis=0)

    fresh = jnp.sum(q.astype(F32) * per_head(new_keys), axis=-1, keepdims=True) * scale
    n = jnp.where(depth == 0, fresh, MASKED)
    level = jnp.floor(jnp.maximum(jnp.max(s, axis=-1, keepdims=True), n))
    w = jnp.where(allowed, jnp.exp2(s - level), 0.0).astype(BF16)
    nw = jnp.where(depth == 0, jnp.exp2(n - level), 0.0).astype(BF16).astype(F32)
    total = jnp.sum(w.astype(F32), axis=-1, keepdims=True) + nw
    added = nw * per_head(new_values)
    column = lax.broadcasted_iota(jnp.int32, (rows, 128), 1)
    stats = jnp.where(column < 64, level, total)
    for p, r in enumerate(order):
        at = slice(p * heads, (p + 1) * heads)
        o = matmul(w[at], side_by_side(values[r]))
        out = own if p < half else other
        out[p % half, 0:8, :] = jnp.where(low8, o[:, 0:width], o[:, width : 2 * width]) + added[at]
        out[p % half, 8:16, :] = stats[at]


def image_kernel(after, arrived, keys, values, out):
    del after
    groups = arrived.shape[0]
    rows = groups * 8
    images, _, patches, width = keys.shape
    scale = 1.0 / (math.sqrt(width) * math.log(2.0))
    q = arrived[:, 0:8, :].reshape(rows, width)
    code = arrived[:, 8:16, :].reshape(rows, width).astype(F32)
    within = jnp.floor(code * 0.5)
    within_lane = within.T[0:1, :]
    low = lax.broadcasted_iota(jnp.int32, (rows, 1), 0) % 8 < 4
    zero = jnp.zeros_like(q)
    both = jnp.concatenate([jnp.where(low, q, zero), jnp.where(low, zero, q)], axis=1)
    across = jnp.zeros((patches, rows), F32)
    for i in range(images):
        across = jnp.where(
            within_lane == float(i), matmul_t(side_by_side(keys[i]), both), across
        )
    s = across.T * scale
    level = jnp.floor(jnp.max(s, axis=-1, keepdims=True))
    w = jnp.exp2(s - level).astype(BF16)
    present = within[:, 0:1] >= 0.0
    total = jnp.where(present, jnp.sum(w.astype(F32), axis=-1, keepdims=True), 0.0)
    nothing = jnp.zeros_like(w)
    o = jnp.zeros((rows, 2 * width), F32)
    for i in range(images):
        o = o + matmul(jnp.where(within[:, 0:1] == float(i), w, nothing), side_by_side(values[i]))
    o = jnp.where(low, o[:, 0:width], o[:, width : 2 * width])
    o = o / jnp.where(present, total, 1.0)
    lane = lax.broadcasted_iota(jnp.int32, (rows, width), 1)
    level_high = level.astype(BF16).astype(F32)
    total_high = total.astype(BF16).astype(F32)
    stats = jnp.where(
        lane < 64,
        jnp.where(lane < 32, level_high, level - level_high),
        jnp.where(lane < 96, total_high, total - total_high),
    )
    second = code - 2.0 * within
    o3 = o.astype(BF16).reshape(groups, 8, width)
    for h in range(2):
        out[:, h, 0:8, :] = o3
        out[:, h, 8:16, :] = (
            jnp.where(second == float(h), stats, 0.0).astype(BF16).reshape(groups, 8, width)
        )


def merge_kernel(plan, back, own, other, states, weight, out, mine, sent, joined, value16, sem):
    half, heads, width = out.shape
    rows = half * heads
    parts = []
    for ref in (own, other):
        stats = ref[:, 8:16, :].reshape(rows, 128)
        parts.append((stats[:, 0:1], stats[:, 64:65], ref[:, 0:8, :].reshape(rows, width)))
    blocks = back[...].reshape(back.shape[0] * 16, width)
    lane = lax.broadcasted_iota(jnp.int32, (rows, blocks.shape[0]), 1)
    head = lax.broadcasted_iota(jnp.int32, (rows, blocks.shape[0]), 0) % heads
    mine_at = pl.ds(pl.multiple_of(rows * lax.axis_index("depth"), rows), rows)
    for k in range(2):
        sender = plan[k, mine_at, :]
        wide = jnp.concatenate([sender] * (blocks.shape[0] // 128), axis=1)
        at = lane - wide * 16 - head
        picks = [jnp.where(at == shift, 1.0, 0.0).astype(BF16) for shift in (0, 8)]
        got = matmul(jnp.concatenate(picks, axis=0), blocks)
        stats = got[rows : 2 * rows]
        total = stats[:, 64:65] + stats[:, 96:97]
        level = jnp.where(sender[:, 0:1] >= 0, stats[:, 0:1] + stats[:, 32:33], MASKED)
        parts.append((level, total, got[0:rows] * total))
    top = functools.reduce(jnp.maximum, [p[0] for p in parts])
    factors = [jnp.exp2(p[0] - top) for p in parts]
    total = sum(f * p[1] for f, p in zip(factors, parts))
    weighted = sum(f * p[2] for f, p in zip(factors, parts))
    value = weighted / total
    joined[...] = value
    value16[...] = value.astype(BF16).reshape(out.shape)
    leave = pltpu.make_async_copy(value16, out, sem)
    leave.start()
    flat = jnp.concatenate(
        [joined[pl.ds(h, half, stride=heads), :] for h in range(heads)], axis=1
    ).astype(BF16)
    row = lax.broadcasted_iota(jnp.int32, (half, 1), 0) - 2 * lax.axis_index("mp")
    step = 512
    for c in range(mine.shape[1] // step):
        at = slice(c * step, (c + 1) * step)
        before = jnp.where(row == 1, states[1:2, at], states[0:1, at]).astype(F32)
        before = jnp.where((row == 0) | (row == 1), before, 0.0)
        value = before + matmul(flat, weight[:, at])
        mine[:, at] = value
        sent[:, at] = value.astype(BF16)
    leave.wait()


def norm_kernel(mine, first, second, third, gain, rest, out):
    x = mine[...] + first[...].astype(F32) + second[...].astype(F32) + third[...].astype(F32)
    position = lax.axis_index("mp")
    kept = x[0:2]
    for c in range(1, x.shape[0] // 2):
        kept = jnp.where(position == c, x[2 * c : 2 * c + 2], kept)
    rest[...] = kept
    spread = jnp.mean(x * x, axis=-1, keepdims=True)
    normed = (x * lax.rsqrt(spread + NORM_EPSILON) * gain[...]).astype(BF16)
    for g in range(out.shape[0]):
        out[g] = normed


def feed_kernel(x, gate, up, down, out, lined):
    a = matmul_t(gate[...], x[...])
    b = matmul_t(up[...], x[...])
    hidden = (a / (1.0 + jnp.exp(-a)) * b).T.astype(BF16)
    tokens = hidden.shape[0]
    tiles = lined.shape[0]
    for q in range(4):
        at = slice(q * tiles * 128, (q + 1) * tiles * 128)
        part = matmul(hidden, down[:, at])
        for c in range(tiles):
            lined[c, pl.ds(q, tokens, stride=4), :] = part[:, c * 128 : (c + 1) * 128]
    for c in range(tiles):
        block = lined[c].astype(BF16).reshape(out.shape[0], 8, 128)
        out[:, :, c * 128 : (c + 1) * 128] = block


def last_kernel(arrived, residual, out):
    total = arrived[0].astype(F32)
    for k in range(1, arrived.shape[0]):
        total = total + arrived[k].astype(F32)
    quarter = arrived.shape[2]
    for t in range(2):
        for q in range(4):
            at = slice(q * quarter, (q + 1) * quarter)
            row = t * 4 + q
            out[t : t + 1, at] = (residual[t : t + 1, at] + total[row : row + 1]).astype(BF16)


def on_device(
    states,
    queries,
    new_keys,
    new_values,
    text_keys,
    text_values,
    text_length,
    image_keys,
    image_values,
    image_slot,
    block_list,
    block_count,
    image_first,
    image_count,
    out_weight,
    norm_gain,
    gate_weight,
    up_weight,
    down_weight,
):
    groups = lax.axis_size("group")
    depths = lax.axis_size("depth")
    ring = lax.axis_size("mp")
    requests, heads, width = queries.shape
    half = requests // depths
    features = states.shape[1]

    integers = (image_slot, block_list, block_count, image_first, image_count)
    in_place = [in_hbm(x) for x in (*integers, queries)]
    routed, plan = call(
        route_kernel,
        (
            jax.ShapeDtypeStruct((groups, 16, width), BF16),
            jax.ShapeDtypeStruct((2, requests * heads, 128), jnp.int32),
        ),
        [HBM] * 6,
        20_000_000_000,
        100_000,
        "route",
        scratch=[pltpu.SMEM(i.shape, jnp.int32) for i in integers]
        + [pltpu.VMEM(queries.shape, BF16), pltpu.SemaphoreType.DMA((len(in_place),))],
        out_specs=(VMEM, VMEM),
    )(*in_place)
    arrived = lax.all_to_all(routed, "group", 0, 0, tiled=True)
    arrived, queries = lax.optimization_barrier((arrived, queries))

    part = jax.ShapeDtypeStruct((half, 16, width), F32)
    own, other = call(
        text_kernel,
        (part, part),
        [HBM] + [VMEM] * 5,
        200_000_000,
        4_400_000,
        "text",
        scratch=[pltpu.SMEM(text_length.shape, jnp.int32), pltpu.SemaphoreType.DMA],
    )(in_hbm(text_length), queries, new_keys, new_values, text_keys, text_values)
    other = lax.ppermute(other, "depth", [(0, 1), (1, 0)])

    back = call(
        image_kernel,
        jax.ShapeDtypeStruct((groups, depths, 16, width), BF16),
        [VMEM] * 4,
        10_000_000_000,
        5_000_000,
        "image",
    )(own, arrived, image_keys, image_values)
    back, other = lax.optimization_barrier((back, other))
    back = lax.all_to_all(
        back.reshape(groups * depths, 16, width), ("group", "depth"), 0, 0, tiled=True
    )
    attention, mine, sent = call(
        merge_kernel,
        (
            jax.ShapeDtypeStruct((half, heads, width), BF16),
            jax.ShapeDtypeStruct((half, features), F32),
            jax.ShapeDtypeStruct((half, features), BF16),
        ),
        [VMEM] * 6,
        100_000_000,
        8_800_000,
        "merge",
        scratch=[
            pltpu.VMEM((half * heads, width), F32),
            pltpu.VMEM((half, heads, width), BF16),
            pltpu.SemaphoreType.DMA,
        ],
        out_specs=(HBM, VMEM, VMEM),
    )(plan, back, own, other, states, out_weight)
    passed = [
        lax.ppermute(sent, "mp", [(i, i ^ k) for i in range(ring)]) for k in (2, 3, 1)
    ]
    rest, normed = call(
        norm_kernel,
        (
            jax.ShapeDtypeStruct((2, features), F32),
            jax.ShapeDtypeStruct((groups, half, features), BF16),
        ),
        [VMEM] * 5,
        10_000_000_000,
        1_600_000,
        "norm",
    )(mine, *passed, norm_gain.reshape(1, features))
    tokens = lax.all_to_all(normed, "group", 0, 0, tiled=True).reshape(groups * half, features)
    peers = groups * ring
    down = call(
        feed_kernel,
        jax.ShapeDtypeStruct((peers, 8, features // 4), BF16),
        [VMEM] * 4,
        1_400_000_000,
        7_000_000,
        "feed",
        scratch=[pltpu.VMEM((features // 512, groups * half * 4, 128), F32)],
    )(tokens, gate_weight.T, up_weight.T, down_weight)
    gathered = lax.all_to_all(down, ("group", "mp"), 0, 0, tiled=True)
    layer_out = call(
        last_kernel,
        jax.ShapeDtypeStruct((2, features), BF16),
        [VMEM] * 2,
        0,
        1_300_000,
        "last",
    )(gathered, rest)
    return attention, layer_out


def solution(mesh):
    placed = (
        P(("group", "depth", "mp"), None),
        P("group", "mp", None),
        P("group", "mp", None),
        P("group", "mp", None),
        P("group", "mp", "depth", None),
        P("group", "mp", "depth", None),
        P("group"),
        P("group", "mp", None, None),
        P("group", "mp", None, None),
        P(),
        P(),
        P(),
        P("group"),
        P("group"),
        P("mp", None),
        P(),
        P(None, ("group", "mp")),
        P(None, ("group", "mp")),
        P(("group", "mp"), None),
    )
    return jax.shard_map(
        on_device,
        mesh=mesh,
        in_specs=placed,
        out_specs=(P(("group", "depth"), "mp", None), P(("group", "depth", "mp"), None)),
        check_vma=False,
    )
```

```python
import functools
import math

import jax
import jax.numpy as jnp
from jax import lax
from jax.experimental import pallas as pl
from jax.experimental.pallas import tpu as pltpu
from jax.sharding import PartitionSpec as P

MASKED = -1e30
NORM_EPSILON = 1e-05
BF16 = jnp.bfloat16
F32 = jnp.float32
VMEM = pl.BlockSpec(memory_space=pltpu.VMEM)
SMEM = pl.BlockSpec(memory_space=pltpu.SMEM)


HBM = pl.BlockSpec(memory_space=pltpu.MemorySpace.HBM)


def call(kernel, out_shape, in_specs, flops, nbytes, name, scratch=(), vmem=16 << 20, out_specs=None):
    return pl.pallas_call(
        kernel,
        out_shape=out_shape,
        in_specs=in_specs,
        out_specs=out_specs or jax.tree.map(lambda _: VMEM, out_shape),
        scratch_shapes=list(scratch),
        cost_estimate=pl.CostEstimate(flops=flops, bytes_accessed=nbytes, transcendentals=0),
        compiler_params=pltpu.CompilerParams(vmem_limit_bytes=vmem),
        name=name,
    )


def in_hbm(x):
    return pltpu.with_memory_space_constraint(x, pltpu.MemorySpace.HBM)


def matmul(a, b):
    return lax.dot_general(a, b, (((1,), (0,)), ((), ())), preferred_element_type=F32)


def matmul_t(a, b):
    return lax.dot_general(a, b, (((1,), (1,)), ((), ())), preferred_element_type=F32)


def route_kernel(
    slots_hbm, blocks_hbm, count_hbm, first_hbm, images_hbm, queries_hbm, out, plan, *scratch
):
    slots, blocks, count, first, images, queries, sems = scratch
    copies = [
        pltpu.make_async_copy(src, dst, sems.at[k])
        for k, (src, dst) in enumerate(
            (
                (first_hbm, first),
                (images_hbm, images),
                (count_hbm, count),
                (blocks_hbm, blocks),
                (slots_hbm, slots),
                (queries_hbm, queries),
            )
        )
    ]
    for copy in copies:
        copy.start()
    group, depth = lax.axis_index("group"), lax.axis_index("depth")
    requests = queries.shape[0]
    half = requests // 2
    out[...] = jnp.full(out.shape, -1.0, BF16)
    for copy in copies:
        copy.wait()
    listed = count[group]

    def source(place):
        slot = slots[blocks[group, jnp.minimum(place, blocks.shape[1] - 1)]]
        return slot >> 3, slot & 7

    for r in range(requests):
        start, read = first[r], images[r]
        for k in range(2):
            place = start + k
            owner, within = source(place)
            live = (k < read) & (place < listed)
            sender = jnp.where(live, owner * 2 + (place & 1), -1)
            plan[k, 8 * r : 8 * r + 8, :] = jnp.full((8, 128), sender, jnp.int32)

            @pl.when(live & ((place & 1) == depth))
            def _():
                out[owner, 0:8, :] = queries[r]
                code = (within * 2 + r // half).astype(F32)
                out[owner, 8:16, :] = jnp.full((8, 128), code, F32).astype(BF16)


def side_by_side(pair):
    return jnp.concatenate([pair[0], pair[1]], axis=1)


def text_kernel(lengths_hbm, queries, new_keys, new_values, keys, values, own, other, lengths, sem):
    fetch = pltpu.make_async_copy(lengths_hbm, lengths, sem)
    fetch.start()
    depth = lax.axis_index("depth")
    requests, heads, width = queries.shape
    half = requests // 2
    rows = requests * heads
    span = keys.shape[2]
    scale = 1.0 / (math.sqrt(width) * math.log(2.0))
    order = [(p + half * depth) % requests for p in range(requests)]
    low8 = lax.broadcasted_iota(jnp.int32, (heads, 1), 0) < heads // 2
    low = lax.broadcasted_iota(jnp.int32, (rows, 1), 0) % heads < heads // 2
    lane = lax.broadcasted_iota(jnp.int32, (1, rows), 1) // heads
    q = jnp.concatenate([queries[r] for r in order], axis=0)
    zero = jnp.zeros_like(q)
    both = jnp.concatenate([jnp.where(low, q, zero), jnp.where(low, zero, q)], axis=1)
    across = jnp.zeros((span, rows), F32)
    for p, r in enumerate(order):
        across = jnp.where(lane == p, matmul_t(side_by_side(keys[r]), both), across)
    fetch.wait()
    length = jnp.concatenate([jnp.full((heads, 1), lengths[r]) for r in order], axis=0)
    where = depth * span + lax.broadcasted_iota(jnp.int32, (rows, span), 1)
    allowed = where < length
    s = jnp.where(allowed, across.T * scale, MASKED)

    def per_head(ref):
        pairs = [ref[r].astype(F32) for r in order]
        return jnp.concatenate([jnp.where(low8, x[0:1], x[1:2]) for x in pairs], axis=0)

    fresh = jnp.sum(q.astype(F32) * per_head(new_keys), axis=-1, keepdims=True) * scale
    n = jnp.where(depth == 0, fresh, MASKED)
    level = jnp.floor(jnp.maximum(jnp.max(s, axis=-1, keepdims=True), n))
    w = jnp.where(allowed, jnp.exp2(s - level), 0.0).astype(BF16)
    nw = jnp.where(depth == 0, jnp.exp2(n - level), 0.0).astype(BF16).astype(F32)
    total = jnp.sum(w.astype(F32), axis=-1, keepdims=True) + nw
    added = nw * per_head(new_values)
    column = lax.broadcasted_iota(jnp.int32, (rows, 128), 1)
    stats = jnp.where(column < 64, level, total)
    for p, r in enumerate(order):
        at = slice(p * heads, (p + 1) * heads)
        o = matmul(w[at], side_by_side(values[r]))
        out = own if p < half else other
        out[p % half, 0:8, :] = jnp.where(low8, o[:, 0:width], o[:, width : 2 * width]) + added[at]
        out[p % half, 8:16, :] = stats[at]


def image_kernel(after, arrived, keys, values, out):
    del after
    groups = arrived.shape[0]
    rows = groups * 8
    images, _, patches, width = keys.shape
    scale = 1.0 / (math.sqrt(width) * math.log(2.0))
    q = arrived[:, 0:8, :].reshape(rows, width)
    code = arrived[:, 8:16, :].reshape(rows, width).astype(F32)
    within = jnp.floor(code * 0.5)
    within_lane = within.T[0:1, :]
    low = lax.broadcasted_iota(jnp.int32, (rows, 1), 0) % 8 < 4
    zero = jnp.zeros_like(q)
    both = jnp.concatenate([jnp.where(low, q, zero), jnp.where(low, zero, q)], axis=1)
    across = jnp.zeros((patches, rows), F32)
    for i in range(images):
        across = jnp.where(
            within_lane == float(i), matmul_t(side_by_side(keys[i]), both), across
        )
    s = across.T * scale
    level = jnp.floor(jnp.max(s, axis=-1, keepdims=True))
    w = jnp.exp2(s - level).astype(BF16)
    present = within[:, 0:1] >= 0.0
    total = jnp.where(present, jnp.sum(w.astype(F32), axis=-1, keepdims=True), 0.0)
    nothing = jnp.zeros_like(w)
    o = jnp.zeros((rows, 2 * width), F32)
    for i in range(images):
        o = o + matmul(jnp.where(within[:, 0:1] == float(i), w, nothing), side_by_side(values[i]))
    o = jnp.where(low, o[:, 0:width], o[:, width : 2 * width])
    o = o / jnp.where(present, total, 1.0)
    lane = lax.broadcasted_iota(jnp.int32, (rows, width), 1)
    level_high = level.astype(BF16).astype(F32)
    total_high = total.astype(BF16).astype(F32)
    stats = jnp.where(
        lane < 64,
        jnp.where(lane < 32, level_high, level - level_high),
        jnp.where(lane < 96, total_high, total - total_high),
    )
    second = code - 2.0 * within
    o3 = o.astype(BF16).reshape(groups, 8, width)
    for h in range(2):
        out[:, h, 0:8, :] = o3
        out[:, h, 8:16, :] = (
            jnp.where(second == float(h), stats, 0.0).astype(BF16).reshape(groups, 8, width)
        )


def merge_kernel(plan, back, own, other, states, weight, out, mine, sent, joined, value16, sem):
    half, heads, width = out.shape
    rows = half * heads
    parts = []
    for ref in (own, other):
        stats = ref[:, 8:16, :].reshape(rows, 128)
        parts.append((stats[:, 0:1], stats[:, 64:65], ref[:, 0:8, :].reshape(rows, width)))
    blocks = back[...].reshape(back.shape[0] * 16, width)
    lane = lax.broadcasted_iota(jnp.int32, (rows, blocks.shape[0]), 1)
    head = lax.broadcasted_iota(jnp.int32, (rows, blocks.shape[0]), 0) % heads
    mine_at = pl.ds(pl.multiple_of(rows * lax.axis_index("depth"), rows), rows)
    for k in range(2):
        sender = plan[k, mine_at, :]
        wide = jnp.concatenate([sender] * (blocks.shape[0] // 128), axis=1)
        at = lane - wide * 16 - head
        picks = [jnp.where(at == shift, 1.0, 0.0).astype(BF16) for shift in (0, 8)]
        got = matmul(jnp.concatenate(picks, axis=0), blocks)
        stats = got[rows : 2 * rows]
        total = stats[:, 64:65] + stats[:, 96:97]
        level = jnp.where(sender[:, 0:1] >= 0, stats[:, 0:1] + stats[:, 32:33], MASKED)
        parts.append((level, total, got[0:rows] * total))
    top = functools.reduce(jnp.maximum, [p[0] for p in parts])
    factors = [jnp.exp2(p[0] - top) for p in parts]
    total = sum(f * p[1] for f, p in zip(factors, parts))
    weighted = sum(f * p[2] for f, p in zip(factors, parts))
    value = weighted / total
    joined[...] = value
    value16[...] = value.astype(BF16).reshape(out.shape)
    leave = pltpu.make_async_copy(value16, out, sem)
    leave.start()
    flat = jnp.concatenate(
        [joined[pl.ds(h, half, stride=heads), :] for h in range(heads)], axis=1
    ).astype(BF16)
    row = lax.broadcasted_iota(jnp.int32, (half, 1), 0) - 2 * lax.axis_index("mp")
    step = 512
    for c in range(mine.shape[1] // step):
        at = slice(c * step, (c + 1) * step)
        before = jnp.where(row == 1, states[1:2, at], states[0:1, at]).astype(F32)
        before = jnp.where((row == 0) | (row == 1), before, 0.0)
        value = before + matmul(flat, weight[:, at])
        mine[:, at] = value
        sent[:, at] = value.astype(BF16)
    leave.wait()


def norm_kernel(mine, first, second, third, gain, rest, out):
    x = mine[...] + first[...].astype(F32) + second[...].astype(F32) + third[...].astype(F32)
    position = lax.axis_index("mp")
    kept = x[0:2]
    for c in range(1, x.shape[0] // 2):
        kept = jnp.where(position == c, x[2 * c : 2 * c + 2], kept)
    rest[...] = kept
    spread = jnp.mean(x * x, axis=-1, keepdims=True)
    normed = (x * lax.rsqrt(spread + NORM_EPSILON) * gain[...]).astype(BF16)
    for g in range(out.shape[0]):
        out[g] = normed


def feed_kernel(x, gate, up, down, out, lined):
    units, deep = gate.shape
    a = jnp.zeros((units, x.shape[0]), F32)
    b = jnp.zeros((units, x.shape[0]), F32)
    for k in range(0, deep, 256):
        piece = x[:, k : k + 256]
        a = a + matmul_t(gate[:, k : k + 256], piece)
        b = b + matmul_t(up[:, k : k + 256], piece)
    hidden = (a / (1.0 + jnp.exp(-a)) * b).T.astype(BF16)
    tokens = hidden.shape[0]
    quarter = out.shape[2]
    for begin in range(0, quarter, 256):
        tiles = range(begin // 128, begin // 128 + 2)
        for q in range(4):
            part = matmul(hidden, down[:, q * quarter + begin : q * quarter + begin + 256])
            for c in tiles:
                at = c * 128 - begin
                lined[c, pl.ds(q, tokens, stride=4), :] = part[:, at : at + 128]
        for c in tiles:
            block = lined[c].astype(BF16).reshape(out.shape[0], 8, 128)
            out[:, :, c * 128 : (c + 1) * 128] = block


def last_kernel(arrived, residual, out):
    total = arrived[0].astype(F32)
    for k in range(1, arrived.shape[0]):
        total = total + arrived[k].astype(F32)
    quarter = arrived.shape[2]
    for t in range(2):
        for q in range(4):
            at = slice(q * quarter, (q + 1) * quarter)
            row = t * 4 + q
            out[t : t + 1, at] = (residual[t : t + 1, at] + total[row : row + 1]).astype(BF16)


def on_device(
    states,
    queries,
    new_keys,
    new_values,
    text_keys,
    text_values,
    text_length,
    image_keys,
    image_values,
    image_slot,
    block_list,
    block_count,
    image_first,
    image_count,
    out_weight,
    norm_gain,
    gate_weight,
    up_weight,
    down_weight,
):
    groups = lax.axis_size("group")
    depths = lax.axis_size("depth")
    ring = lax.axis_size("mp")
    requests, heads, width = queries.shape
    half = requests // depths
    features = states.shape[1]

    integers = (image_slot, block_list, block_count, image_first, image_count)
    in_place = [in_hbm(x) for x in (*integers, queries)]
    routed, plan = call(
        route_kernel,
        (
            jax.ShapeDtypeStruct((groups, 16, width), BF16),
            jax.ShapeDtypeStruct((2, requests * heads, 128), jnp.int32),
        ),
        [HBM] * 6,
        20_000_000_000,
        100_000,
        "route",
        scratch=[pltpu.SMEM(i.shape, jnp.int32) for i in integers]
        + [pltpu.VMEM(queries.shape, BF16), pltpu.SemaphoreType.DMA((len(in_place),))],
        out_specs=(VMEM, VMEM),
    )(*in_place)
    arrived = lax.all_to_all(routed, "group", 0, 0, tiled=True)
    arrived, queries = lax.optimization_barrier((arrived, queries))

    part = jax.ShapeDtypeStruct((half, 16, width), F32)
    own, other = call(
        text_kernel,
        (part, part),
        [HBM] + [VMEM] * 5,
        200_000_000,
        4_400_000,
        "text",
        scratch=[pltpu.SMEM(text_length.shape, jnp.int32), pltpu.SemaphoreType.DMA],
    )(in_hbm(text_length), queries, new_keys, new_values, text_keys, text_values)
    other = lax.ppermute(other, "depth", [(0, 1), (1, 0)])

    back = call(
        image_kernel,
        jax.ShapeDtypeStruct((groups, depths, 16, width), BF16),
        [VMEM] * 4,
        10_000_000_000,
        5_000_000,
        "image",
    )(own, arrived, image_keys, image_values)
    back, other = lax.optimization_barrier((back, other))
    back = lax.all_to_all(
        back.reshape(groups * depths, 16, width), ("group", "depth"), 0, 0, tiled=True
    )
    attention, mine, sent = call(
        merge_kernel,
        (
            jax.ShapeDtypeStruct((half, heads, width), BF16),
            jax.ShapeDtypeStruct((half, features), F32),
            jax.ShapeDtypeStruct((half, features), BF16),
        ),
        [VMEM] * 6,
        10_000_000_000,
        8_800_000,
        "merge",
        scratch=[
            pltpu.VMEM((half * heads, width), F32),
            pltpu.VMEM((half, heads, width), BF16),
            pltpu.SemaphoreType.DMA,
        ],
        out_specs=(HBM, VMEM, VMEM),
    )(plan, back, own, other, states, out_weight)
    passed = [
        lax.ppermute(sent, "mp", [(i, i ^ k) for i in range(ring)]) for k in (2, 3, 1)
    ]
    rest, normed = call(
        norm_kernel,
        (
            jax.ShapeDtypeStruct((2, features), F32),
            jax.ShapeDtypeStruct((groups, half, features), BF16),
        ),
        [VMEM] * 5,
        0,
        1_600_000,
        "norm",
    )(mine, *passed, norm_gain.reshape(1, features))
    tokens = lax.all_to_all(normed, "group", 0, 0, tiled=True).reshape(groups * half, features)
    peers = groups * ring
    down = call(
        feed_kernel,
        jax.ShapeDtypeStruct((peers, 8, features // 4), BF16),
        [VMEM] * 4,
        1_400_000_000,
        7_000_000,
        "feed",
        scratch=[pltpu.VMEM((features // 512, groups * half * 4, 128), F32)],
    )(tokens, gate_weight.T, up_weight.T, down_weight)
    gathered = lax.all_to_all(down, ("group", "mp"), 0, 0, tiled=True)
    layer_out = call(
        last_kernel,
        jax.ShapeDtypeStruct((2, features), BF16),
        [VMEM] * 2,
        0,
        1_300_000,
        "last",
    )(gathered, rest)
    return attention, layer_out


def solution(mesh):
    placed = (
        P(("group", "depth", "mp"), None),
        P("group", "mp", None),
        P("group", "mp", None),
        P("group", "mp", None),
        P("group", "mp", "depth", None),
        P("group", "mp", "depth", None),
        P("group"),
        P("group", "mp", None, None),
        P("group", "mp", None, None),
        P(),
        P(),
        P(),
        P("group"),
        P("group"),
        P("mp", None),
        P(),
        P(None, ("group", "mp")),
        P(None, ("group", "mp")),
        P(("group", "mp"), None),
    )
    return jax.shard_map(
        on_device,
        mesh=mesh,
        in_specs=placed,
        out_specs=(P(("group", "depth"), "mp", None), P(("group", "depth", "mp"), None)),
        check_vma=False,
    )
```

```python
import functools
import math

import jax
import jax.numpy as jnp
from jax import lax
from jax.experimental import pallas as pl
from jax.experimental.pallas import tpu as pltpu
from jax.sharding import PartitionSpec as P

MASKED = -1e30
NORM_EPSILON = 1e-05
BF16 = jnp.bfloat16
F32 = jnp.float32
VMEM = pl.BlockSpec(memory_space=pltpu.VMEM)
SMEM = pl.BlockSpec(memory_space=pltpu.SMEM)


HBM = pl.BlockSpec(memory_space=pltpu.MemorySpace.HBM)


def call(kernel, out_shape, in_specs, flops, nbytes, name, scratch=(), vmem=16 << 20, out_specs=None):
    return pl.pallas_call(
        kernel,
        out_shape=out_shape,
        in_specs=in_specs,
        out_specs=out_specs or jax.tree.map(lambda _: VMEM, out_shape),
        scratch_shapes=list(scratch),
        cost_estimate=pl.CostEstimate(flops=flops, bytes_accessed=nbytes, transcendentals=0),
        compiler_params=pltpu.CompilerParams(vmem_limit_bytes=vmem),
        name=name,
    )


def in_hbm(x):
    return pltpu.with_memory_space_constraint(x, pltpu.MemorySpace.HBM)


def matmul(a, b):
    return lax.dot_general(a, b, (((1,), (0,)), ((), ())), preferred_element_type=F32)


def matmul_t(a, b):
    return lax.dot_general(a, b, (((1,), (1,)), ((), ())), preferred_element_type=F32)


def route_kernel(
    slots_hbm, blocks_hbm, count_hbm, first_hbm, images_hbm, queries_hbm, out, plan, *scratch
):
    slots, blocks, count, first, images, queries, sems = scratch
    copies = [
        pltpu.make_async_copy(src, dst, sems.at[k])
        for k, (src, dst) in enumerate(
            (
                (first_hbm, first),
                (images_hbm, images),
                (count_hbm, count),
                (blocks_hbm, blocks),
                (slots_hbm, slots),
                (queries_hbm, queries),
            )
        )
    ]
    for copy in copies:
        copy.start()
    group, depth = lax.axis_index("group"), lax.axis_index("depth")
    requests = queries.shape[0]
    half = requests // 2
    out[...] = jnp.full(out.shape, -1.0, BF16)
    for copy in copies:
        copy.wait()
    listed = count[group]

    def source(place):
        slot = slots[blocks[group, jnp.minimum(place, blocks.shape[1] - 1)]]
        return slot >> 3, slot & 7

    for r in range(requests):
        start, read = first[r], images[r]
        for k in range(2):
            place = start + k
            owner, within = source(place)
            live = (k < read) & (place < listed)
            sender = jnp.where(live, owner * 2 + (place & 1), -1)
            plan[k, 8 * r : 8 * r + 8, :] = jnp.full((8, 128), sender, jnp.int32)

            @pl.when(live & ((place & 1) == depth))
            def _():
                out[owner, 0:8, :] = queries[r]
                code = (within * 2 + r // half).astype(F32)
                out[owner, 8:16, :] = jnp.full((8, 128), code, F32).astype(BF16)


def side_by_side(pair):
    return jnp.concatenate([pair[0], pair[1]], axis=1)


def text_kernel(lengths_hbm, queries, new_keys, new_values, keys, values, own, other, lengths, sem):
    fetch = pltpu.make_async_copy(lengths_hbm, lengths, sem)
    fetch.start()
    depth = lax.axis_index("depth")
    requests, heads, width = queries.shape
    half = requests // 2
    rows = requests * heads
    span = keys.shape[2]
    scale = 1.0 / (math.sqrt(width) * math.log(2.0))
    order = [(p + half * depth) % requests for p in range(requests)]
    low8 = lax.broadcasted_iota(jnp.int32, (heads, 1), 0) < heads // 2
    low = lax.broadcasted_iota(jnp.int32, (rows, 1), 0) % heads < heads // 2
    lane = lax.broadcasted_iota(jnp.int32, (1, rows), 1) // heads
    q = jnp.concatenate([queries[r] for r in order], axis=0)
    zero = jnp.zeros_like(q)
    both = jnp.concatenate([jnp.where(low, q, zero), jnp.where(low, zero, q)], axis=1)
    across = jnp.zeros((span, rows), F32)
    for p, r in enumerate(order):
        across = jnp.where(lane == p, matmul_t(side_by_side(keys[r]), both), across)
    fetch.wait()
    length = jnp.concatenate([jnp.full((heads, 1), lengths[r]) for r in order], axis=0)
    where = depth * span + lax.broadcasted_iota(jnp.int32, (rows, span), 1)
    allowed = where < length
    s = jnp.where(allowed, across.T * scale, MASKED)

    def per_head(ref):
        pairs = [ref[r].astype(F32) for r in order]
        return jnp.concatenate([jnp.where(low8, x[0:1], x[1:2]) for x in pairs], axis=0)

    fresh = jnp.sum(q.astype(F32) * per_head(new_keys), axis=-1, keepdims=True) * scale
    n = jnp.where(depth == 0, fresh, MASKED)
    level = jnp.floor(jnp.maximum(jnp.max(s, axis=-1, keepdims=True), n))
    w = jnp.where(allowed, jnp.exp2(s - level), 0.0).astype(BF16)
    nw = jnp.where(depth == 0, jnp.exp2(n - level), 0.0).astype(BF16).astype(F32)
    total = jnp.sum(w.astype(F32), axis=-1, keepdims=True) + nw
    added = nw * per_head(new_values)
    column = lax.broadcasted_iota(jnp.int32, (rows, 128), 1)
    stats = jnp.where(column < 64, level, total)
    for p, r in enumerate(order):
        at = slice(p * heads, (p + 1) * heads)
        o = matmul(w[at], side_by_side(values[r]))
        out = own if p < half else other
        out[p % half, 0:8, :] = jnp.where(low8, o[:, 0:width], o[:, width : 2 * width]) + added[at]
        out[p % half, 8:16, :] = stats[at]


def image_kernel(after, arrived, keys, values, out):
    del after
    groups = arrived.shape[0]
    rows = groups * 8
    images, _, patches, width = keys.shape
    scale = 1.0 / (math.sqrt(width) * math.log(2.0))
    q = arrived[:, 0:8, :].reshape(rows, width)
    code = arrived[:, 8:16, :].reshape(rows, width).astype(F32)
    within = jnp.floor(code * 0.5)
    within_lane = within.T[0:1, :]
    low = lax.broadcasted_iota(jnp.int32, (rows, 1), 0) % 8 < 4
    zero = jnp.zeros_like(q)
    both = jnp.concatenate([jnp.where(low, q, zero), jnp.where(low, zero, q)], axis=1)
    across = jnp.zeros((patches, rows), F32)
    for i in range(images):
        across = jnp.where(
            within_lane == float(i), matmul_t(side_by_side(keys[i]), both), across
        )
    s = across.T * scale
    level = jnp.floor(jnp.max(s, axis=-1, keepdims=True))
    w = jnp.exp2(s - level).astype(BF16)
    present = within[:, 0:1] >= 0.0
    total = jnp.where(present, jnp.sum(w.astype(F32), axis=-1, keepdims=True), 0.0)
    o = jnp.zeros((rows, 2 * width), F32)
    for i in range(images):
        o = jnp.where(within[:, 0:1] == float(i), matmul(w, side_by_side(values[i])), o)
    o = jnp.where(low, o[:, 0:width], o[:, width : 2 * width])
    o = o / jnp.where(present, total, 1.0)
    lane = lax.broadcasted_iota(jnp.int32, (rows, width), 1)
    level_high = level.astype(BF16).astype(F32)
    total_high = total.astype(BF16).astype(F32)
    stats = jnp.where(
        lane < 64,
        jnp.where(lane < 32, level_high, level - level_high),
        jnp.where(lane < 96, total_high, total - total_high),
    )
    second = code - 2.0 * within
    o3 = o.astype(BF16).reshape(groups, 8, width)
    for h in range(2):
        out[:, h, 0:8, :] = o3
        out[:, h, 8:16, :] = (
            jnp.where(second == float(h), stats, 0.0).astype(BF16).reshape(groups, 8, width)
        )


def merge_kernel(plan, back, own, other, states, weight, out, mine, sent, joined, value16, sem):
    half, heads, width = out.shape
    rows = half * heads
    parts = []
    for ref in (own, other):
        stats = ref[:, 8:16, :].reshape(rows, 128)
        parts.append((stats[:, 0:1], stats[:, 64:65], ref[:, 0:8, :].reshape(rows, width)))
    blocks = back[...].reshape(back.shape[0] * 16, width)
    lane = lax.broadcasted_iota(jnp.int32, (rows, blocks.shape[0]), 1)
    head = lax.broadcasted_iota(jnp.int32, (rows, blocks.shape[0]), 0) % heads
    mine_at = pl.ds(pl.multiple_of(rows * lax.axis_index("depth"), rows), rows)
    for k in range(2):
        sender = plan[k, mine_at, :]
        wide = jnp.concatenate([sender] * (blocks.shape[0] // 128), axis=1)
        at = lane - wide * 16 - head
        picks = [jnp.where(at == shift, 1.0, 0.0).astype(BF16) for shift in (0, 8)]
        got = matmul(jnp.concatenate(picks, axis=0), blocks)
        stats = got[rows : 2 * rows]
        total = stats[:, 64:65] + stats[:, 96:97]
        level = jnp.where(sender[:, 0:1] >= 0, stats[:, 0:1] + stats[:, 32:33], MASKED)
        parts.append((level, total, got[0:rows] * total))
    top = functools.reduce(jnp.maximum, [p[0] for p in parts])
    factors = [jnp.exp2(p[0] - top) for p in parts]
    total = sum(f * p[1] for f, p in zip(factors, parts))
    weighted = sum(f * p[2] for f, p in zip(factors, parts))
    value = weighted / total
    joined[...] = value
    value16[...] = value.astype(BF16).reshape(out.shape)
    leave = pltpu.make_async_copy(value16, out, sem)
    leave.start()
    flat = jnp.concatenate(
        [joined[pl.ds(h, half, stride=heads), :] for h in range(heads)], axis=1
    ).astype(BF16)
    row = lax.broadcasted_iota(jnp.int32, (half, 1), 0) - 2 * lax.axis_index("mp")
    step = 512
    for c in range(mine.shape[1] // step):
        at = slice(c * step, (c + 1) * step)
        before = jnp.where(row == 1, states[1:2, at], states[0:1, at]).astype(F32)
        before = jnp.where((row == 0) | (row == 1), before, 0.0)
        value = before + matmul(flat, weight[:, at])
        mine[:, at] = value
        sent[:, at] = value.astype(BF16)
    leave.wait()


def norm_kernel(mine, first, second, third, gain, rest, out):
    x = mine[...] + first[...].astype(F32) + second[...].astype(F32) + third[...].astype(F32)
    position = lax.axis_index("mp")
    kept = x[0:2]
    for c in range(1, x.shape[0] // 2):
        kept = jnp.where(position == c, x[2 * c : 2 * c + 2], kept)
    rest[...] = kept
    spread = jnp.mean(x * x, axis=-1, keepdims=True)
    normed = (x * lax.rsqrt(spread + NORM_EPSILON) * gain[...]).astype(BF16)
    for g in range(out.shape[0]):
        out[g] = normed


def feed_kernel(x, gate, up, down, out, lined):
    units, deep = gate.shape
    a = jnp.zeros((units, x.shape[0]), F32)
    b = jnp.zeros((units, x.shape[0]), F32)
    for k in range(0, deep, 256):
        piece = x[:, k : k + 256]
        a = a + matmul_t(gate[:, k : k + 256], piece)
        b = b + matmul_t(up[:, k : k + 256], piece)
    hidden = (a / (1.0 + jnp.exp(-a)) * b).T.astype(BF16)
    tokens = hidden.shape[0]
    quarter = out.shape[2]
    for begin in range(0, quarter, 256):
        tiles = range(begin // 128, begin // 128 + 2)
        for q in range(4):
            part = matmul(hidden, down[:, q * quarter + begin : q * quarter + begin + 256])
            for c in tiles:
                at = c * 128 - begin
                lined[c, pl.ds(q, tokens, stride=4), :] = part[:, at : at + 128]
        for c in tiles:
            block = lined[c].astype(BF16).reshape(out.shape[0], 8, 128)
            out[:, :, c * 128 : (c + 1) * 128] = block


def last_kernel(arrived, residual, out):
    total = arrived[0].astype(F32)
    for k in range(1, arrived.shape[0]):
        total = total + arrived[k].astype(F32)
    quarter = arrived.shape[2]
    for t in range(2):
        for q in range(4):
            at = slice(q * quarter, (q + 1) * quarter)
            row = t * 4 + q
            out[t : t + 1, at] = (residual[t : t + 1, at] + total[row : row + 1]).astype(BF16)


def on_device(
    states,
    queries,
    new_keys,
    new_values,
    text_keys,
    text_values,
    text_length,
    image_keys,
    image_values,
    image_slot,
    block_list,
    block_count,
    image_first,
    image_count,
    out_weight,
    norm_gain,
    gate_weight,
    up_weight,
    down_weight,
):
    groups = lax.axis_size("group")
    depths = lax.axis_size("depth")
    ring = lax.axis_size("mp")
    requests, heads, width = queries.shape
    half = requests // depths
    features = states.shape[1]

    integers = (image_slot, block_list, block_count, image_first, image_count)
    in_place = [in_hbm(x) for x in (*integers, queries)]
    routed, plan = call(
        route_kernel,
        (
            jax.ShapeDtypeStruct((groups, 16, width), BF16),
            jax.ShapeDtypeStruct((2, requests * heads, 128), jnp.int32),
        ),
        [HBM] * 6,
        20_000_000_000,
        100_000,
        "route",
        scratch=[pltpu.SMEM(i.shape, jnp.int32) for i in integers]
        + [pltpu.VMEM(queries.shape, BF16), pltpu.SemaphoreType.DMA((len(in_place),))],
        out_specs=(VMEM, VMEM),
    )(*in_place)
    arrived = lax.all_to_all(routed, "group", 0, 0, tiled=True)
    arrived, queries = lax.optimization_barrier((arrived, queries))

    part = jax.ShapeDtypeStruct((half, 16, width), F32)
    own, other = call(
        text_kernel,
        (part, part),
        [HBM] + [VMEM] * 5,
        200_000_000,
        4_400_000,
        "text",
        scratch=[pltpu.SMEM(text_length.shape, jnp.int32), pltpu.SemaphoreType.DMA],
    )(in_hbm(text_length), queries, new_keys, new_values, text_keys, text_values)
    other = lax.ppermute(other, "depth", [(0, 1), (1, 0)])

    back = call(
        image_kernel,
        jax.ShapeDtypeStruct((groups, depths, 16, width), BF16),
        [VMEM] * 4,
        10_000_000_000,
        5_000_000,
        "image",
    )(own, arrived, image_keys, image_values)
    back, other = lax.optimization_barrier((back, other))
    back = lax.all_to_all(
        back.reshape(groups * depths, 16, width), ("group", "depth"), 0, 0, tiled=True
    )
    attention, mine, sent = call(
        merge_kernel,
        (
            jax.ShapeDtypeStruct((half, heads, width), BF16),
            jax.ShapeDtypeStruct((half, features), F32),
            jax.ShapeDtypeStruct((half, features), BF16),
        ),
        [VMEM] * 6,
        10_000_000_000,
        8_800_000,
        "merge",
        scratch=[
            pltpu.VMEM((half * heads, width), F32),
            pltpu.VMEM((half, heads, width), BF16),
            pltpu.SemaphoreType.DMA,
        ],
        out_specs=(HBM, VMEM, VMEM),
    )(plan, back, own, other, states, out_weight)
    passed = [
        lax.ppermute(sent, "mp", [(i, i ^ k) for i in range(ring)]) for k in (2, 3, 1)
    ]
    rest, normed = call(
        norm_kernel,
        (
            jax.ShapeDtypeStruct((2, features), F32),
            jax.ShapeDtypeStruct((groups, half, features), BF16),
        ),
        [VMEM] * 5,
        0,
        1_600_000,
        "norm",
    )(mine, *passed, norm_gain.reshape(1, features))
    tokens = lax.all_to_all(normed, "group", 0, 0, tiled=True).reshape(groups * half, features)
    peers = groups * ring
    down = call(
        feed_kernel,
        jax.ShapeDtypeStruct((peers, 8, features // 4), BF16),
        [VMEM] * 4,
        1_400_000_000,
        7_000_000,
        "feed",
        scratch=[pltpu.VMEM((features // 512, groups * half * 4, 128), F32)],
    )(tokens, gate_weight.T, up_weight.T, down_weight)
    gathered = lax.all_to_all(down, ("group", "mp"), 0, 0, tiled=True)
    layer_out = call(
        last_kernel,
        jax.ShapeDtypeStruct((2, features), BF16),
        [VMEM] * 2,
        0,
        1_300_000,
        "last",
    )(gathered, rest)
    return attention, layer_out


def solution(mesh):
    placed = (
        P(("group", "depth", "mp"), None),
        P("group", "mp", None),
        P("group", "mp", None),
        P("group", "mp", None),
        P("group", "mp", "depth", None),
        P("group", "mp", "depth", None),
        P("group"),
        P("group", "mp", None, None),
        P("group", "mp", None, None),
        P(),
        P(),
        P(),
        P("group"),
        P("group"),
        P("mp", None),
        P(),
        P(None, ("group", "mp")),
        P(None, ("group", "mp")),
        P(("group", "mp"), None),
    )
    return jax.shard_map(
        on_device,
        mesh=mesh,
        in_specs=placed,
        out_specs=(P(("group", "depth"), "mp", None), P(("group", "depth", "mp"), None)),
        check_vma=False,
    )
```

```python
import functools
import math

import jax
import jax.numpy as jnp
from jax import lax
from jax.experimental import pallas as pl
from jax.experimental.pallas import tpu as pltpu
from jax.sharding import PartitionSpec as P

MASKED = -1e30
NORM_EPSILON = 1e-05
BF16 = jnp.bfloat16
F32 = jnp.float32
VMEM = pl.BlockSpec(memory_space=pltpu.VMEM)
SMEM = pl.BlockSpec(memory_space=pltpu.SMEM)


HBM = pl.BlockSpec(memory_space=pltpu.MemorySpace.HBM)


def call(kernel, out_shape, in_specs, flops, nbytes, name, scratch=(), vmem=16 << 20, out_specs=None):
    return pl.pallas_call(
        kernel,
        out_shape=out_shape,
        in_specs=in_specs,
        out_specs=out_specs or jax.tree.map(lambda _: VMEM, out_shape),
        scratch_shapes=list(scratch),
        cost_estimate=pl.CostEstimate(flops=flops, bytes_accessed=nbytes, transcendentals=0),
        compiler_params=pltpu.CompilerParams(vmem_limit_bytes=vmem),
        name=name,
    )


def in_hbm(x):
    return pltpu.with_memory_space_constraint(x, pltpu.MemorySpace.HBM)


def matmul(a, b):
    return lax.dot_general(a, b, (((1,), (0,)), ((), ())), preferred_element_type=F32)


def matmul_t(a, b):
    return lax.dot_general(a, b, (((1,), (1,)), ((), ())), preferred_element_type=F32)


def route_kernel(
    slots_hbm, blocks_hbm, count_hbm, first_hbm, images_hbm, queries_hbm, out, plan, *scratch
):
    slots, blocks, count, first, images, queries, sems = scratch
    copies = [
        pltpu.make_async_copy(src, dst, sems.at[k])
        for k, (src, dst) in enumerate(
            (
                (first_hbm, first),
                (images_hbm, images),
                (count_hbm, count),
                (blocks_hbm, blocks),
                (slots_hbm, slots),
                (queries_hbm, queries),
            )
        )
    ]
    for copy in copies:
        copy.start()
    group, depth = lax.axis_index("group"), lax.axis_index("depth")
    requests = queries.shape[0]
    half = requests // 2
    out[...] = jnp.full(out.shape, -1.0, BF16)
    for copy in copies:
        copy.wait()
    listed = count[group]

    def source(place):
        slot = slots[blocks[group, jnp.minimum(place, blocks.shape[1] - 1)]]
        return slot >> 3, slot & 7

    for r in range(requests):
        start, read = first[r], images[r]
        for k in range(2):
            place = start + k
            owner, within = source(place)
            live = (k < read) & (place < listed)
            sender = jnp.where(live, owner * 2 + (place & 1), -1)
            plan[k, 8 * r : 8 * r + 8, :] = jnp.full((8, 128), sender, jnp.int32)

            @pl.when(live & ((place & 1) == depth))
            def _():
                out[owner, 0:8, :] = queries[r]
                code = (within * 2 + r // half).astype(F32)
                out[owner, 8:16, :] = jnp.full((8, 128), code, F32).astype(BF16)


def side_by_side(pair):
    return jnp.concatenate([pair[0], pair[1]], axis=1)


def text_kernel(lengths_hbm, queries, new_keys, new_values, keys, values, own, other, lengths, sem):
    fetch = pltpu.make_async_copy(lengths_hbm, lengths, sem)
    fetch.start()
    depth = lax.axis_index("depth")
    requests, heads, width = queries.shape
    half = requests // 2
    rows = requests * heads
    span = keys.shape[2]
    scale = 1.0 / (math.sqrt(width) * math.log(2.0))
    order = [(p + half * depth) % requests for p in range(requests)]
    low8 = lax.broadcasted_iota(jnp.int32, (heads, 1), 0) < heads // 2
    low = lax.broadcasted_iota(jnp.int32, (rows, 1), 0) % heads < heads // 2
    lane = lax.broadcasted_iota(jnp.int32, (1, rows), 1) // heads
    q = jnp.concatenate([queries[r] for r in order], axis=0)
    zero = jnp.zeros_like(q)
    both = jnp.concatenate([jnp.where(low, q, zero), jnp.where(low, zero, q)], axis=1)
    across = jnp.zeros((span, rows), F32)
    for p, r in enumerate(order):
        across = jnp.where(lane == p, matmul_t(side_by_side(keys[r]), both), across)
    fetch.wait()
    length = jnp.concatenate([jnp.full((heads, 1), lengths[r]) for r in order], axis=0)
    where = depth * span + lax.broadcasted_iota(jnp.int32, (rows, span), 1)
    allowed = where < length
    s = jnp.where(allowed, across.T * scale, MASKED)

    def per_head(ref):
        pairs = [ref[r].astype(F32) for r in order]
        return jnp.concatenate([jnp.where(low8, x[0:1], x[1:2]) for x in pairs], axis=0)

    fresh = jnp.sum(q.astype(F32) * per_head(new_keys), axis=-1, keepdims=True) * scale
    n = jnp.where(depth == 0, fresh, MASKED)
    level = jnp.floor(jnp.maximum(jnp.max(s, axis=-1, keepdims=True), n))
    w = jnp.where(allowed, jnp.exp2(s - level), 0.0).astype(BF16)
    nw = jnp.where(depth == 0, jnp.exp2(n - level), 0.0).astype(BF16).astype(F32)
    total = jnp.sum(w.astype(F32), axis=-1, keepdims=True) + nw
    added = nw * per_head(new_values)
    column = lax.broadcasted_iota(jnp.int32, (rows, 128), 1)
    stats = jnp.where(column < 64, level, total)
    for p, r in enumerate(order):
        at = slice(p * heads, (p + 1) * heads)
        o = matmul(w[at], side_by_side(values[r]))
        out = own if p < half else other
        out[p % half, 0:8, :] = jnp.where(low8, o[:, 0:width], o[:, width : 2 * width]) + added[at]
        out[p % half, 8:16, :] = stats[at]


def image_kernel(after, arrived, keys, values, out):
    del after
    groups = arrived.shape[0]
    rows = groups * 8
    images, _, patches, width = keys.shape
    scale = 1.0 / (math.sqrt(width) * math.log(2.0))
    q = arrived[:, 0:8, :].reshape(rows, width)
    code = arrived[:, 8:16, :].reshape(rows, width).astype(F32)
    within = jnp.floor(code * 0.5)
    within_lane = within.T[0:1, :]
    low = lax.broadcasted_iota(jnp.int32, (rows, 1), 0) % 8 < 4
    zero = jnp.zeros_like(q)
    both = jnp.concatenate([jnp.where(low, q, zero), jnp.where(low, zero, q)], axis=1)
    pieces = []
    for begin in range(0, patches, patches // 4):
        at = slice(begin, begin + patches // 4)
        piece = jnp.zeros((patches // 4, rows), F32)
        for i in range(images):
            pair = jnp.concatenate([keys[i, 0, at, :], keys[i, 1, at, :]], axis=1)
            piece = jnp.where(within_lane == float(i), matmul_t(pair, both), piece)
        pieces.append(piece * scale)
    tops = [jnp.max(piece, axis=0, keepdims=True) for piece in pieces]
    level = jnp.floor(functools.reduce(jnp.maximum, tops))
    parts = [jnp.exp2(piece - level).astype(BF16) for piece in pieces]
    total = sum(jnp.sum(part.astype(F32), axis=0, keepdims=True) for part in parts)
    w = jnp.concatenate(parts, axis=0).T
    side = lax.broadcasted_iota(jnp.int32, (width, rows), 0)
    columns = jnp.where(side < 64, level, total).T
    present = within[:, 0:1] >= 0.0
    level = columns[:, 0:1]
    total = jnp.where(present, columns[:, 64:65], 0.0)
    o = jnp.zeros((rows, 2 * width), F32)
    for i in range(images):
        o = jnp.where(within[:, 0:1] == float(i), matmul(w, side_by_side(values[i])), o)
    o = jnp.where(low, o[:, 0:width], o[:, width : 2 * width])
    o = o / jnp.where(present, total, 1.0)
    lane = lax.broadcasted_iota(jnp.int32, (rows, width), 1)
    level_high = level.astype(BF16).astype(F32)
    total_high = total.astype(BF16).astype(F32)
    stats = jnp.where(
        lane < 64,
        jnp.where(lane < 32, level_high, level - level_high),
        jnp.where(lane < 96, total_high, total - total_high),
    )
    second = code - 2.0 * within
    o3 = o.astype(BF16).reshape(groups, 8, width)
    for h in range(2):
        out[:, h, 0:8, :] = o3
        out[:, h, 8:16, :] = (
            jnp.where(second == float(h), stats, 0.0).astype(BF16).reshape(groups, 8, width)
        )


def merge_kernel(plan, back, own, other, states, weight, out, mine, sent, joined, value16, sem):
    half, heads, width = out.shape
    rows = half * heads
    parts = []
    for ref in (own, other):
        stats = ref[:, 8:16, :].reshape(rows, 128)
        parts.append((stats[:, 0:1], stats[:, 64:65], ref[:, 0:8, :].reshape(rows, width)))
    blocks = back[...].reshape(back.shape[0] * 16, width)
    lane = lax.broadcasted_iota(jnp.int32, (rows, blocks.shape[0]), 1)
    head = lax.broadcasted_iota(jnp.int32, (rows, blocks.shape[0]), 0) % heads
    mine_at = pl.ds(pl.multiple_of(rows * lax.axis_index("depth"), rows), rows)
    for k in range(2):
        sender = plan[k, mine_at, :]
        wide = jnp.concatenate([sender] * (blocks.shape[0] // 128), axis=1)
        at = lane - wide * 16 - head
        picks = [jnp.where(at == shift, 1.0, 0.0).astype(BF16) for shift in (0, 8)]
        got = matmul(jnp.concatenate(picks, axis=0), blocks)
        stats = got[rows : 2 * rows]
        total = stats[:, 64:65] + stats[:, 96:97]
        level = jnp.where(sender[:, 0:1] >= 0, stats[:, 0:1] + stats[:, 32:33], MASKED)
        parts.append((level, total, got[0:rows] * total))
    top = functools.reduce(jnp.maximum, [p[0] for p in parts])
    factors = [jnp.exp2(p[0] - top) for p in parts]
    total = sum(f * p[1] for f, p in zip(factors, parts))
    weighted = sum(f * p[2] for f, p in zip(factors, parts))
    value = weighted / total
    joined[...] = value
    value16[...] = value.astype(BF16).reshape(out.shape)
    leave = pltpu.make_async_copy(value16, out, sem)
    leave.start()
    flat = jnp.concatenate(
        [joined[pl.ds(h, half, stride=heads), :] for h in range(heads)], axis=1
    ).astype(BF16)
    row = lax.broadcasted_iota(jnp.int32, (half, 1), 0) - 2 * lax.axis_index("mp")
    step = 512
    for c in range(mine.shape[1] // step):
        at = slice(c * step, (c + 1) * step)
        before = jnp.where(row == 1, states[1:2, at], states[0:1, at]).astype(F32)
        before = jnp.where((row == 0) | (row == 1), before, 0.0)
        value = before + matmul(flat, weight[:, at])
        mine[:, at] = value
        sent[:, at] = value.astype(BF16)
    leave.wait()


def norm_kernel(mine, first, second, third, gain, rest, out):
    x = mine[...] + first[...].astype(F32) + second[...].astype(F32) + third[...].astype(F32)
    position = lax.axis_index("mp")
    kept = x[0:2]
    for c in range(1, x.shape[0] // 2):
        kept = jnp.where(position == c, x[2 * c : 2 * c + 2], kept)
    rest[...] = kept
    spread = jnp.mean(x * x, axis=-1, keepdims=True)
    normed = (x * lax.rsqrt(spread + NORM_EPSILON) * gain[...]).astype(BF16)
    for g in range(out.shape[0]):
        out[g] = normed


def feed_kernel(x, gate, up, down, out, lined):
    units, deep = gate.shape
    a = jnp.zeros((units, x.shape[0]), F32)
    b = jnp.zeros((units, x.shape[0]), F32)
    for k in range(0, deep, 256):
        piece = x[:, k : k + 256]
        a = a + matmul_t(gate[:, k : k + 256], piece)
        b = b + matmul_t(up[:, k : k + 256], piece)
    hidden = (a / (1.0 + jnp.exp(-a)) * b).T.astype(BF16)
    tokens = hidden.shape[0]
    quarter = out.shape[2]
    for begin in range(0, quarter, 256):
        tiles = range(begin // 128, begin // 128 + 2)
        for q in range(4):
            part = matmul(hidden, down[:, q * quarter + begin : q * quarter + begin + 256])
            for c in tiles:
                at = c * 128 - begin
                lined[c, pl.ds(q, tokens, stride=4), :] = part[:, at : at + 128]
        for c in tiles:
            block = lined[c].astype(BF16).reshape(out.shape[0], 8, 128)
            out[:, :, c * 128 : (c + 1) * 128] = block


def last_kernel(arrived, residual, out):
    total = arrived[0].astype(F32)
    for k in range(1, arrived.shape[0]):
        total = total + arrived[k].astype(F32)
    quarter = arrived.shape[2]
    for t in range(2):
        for q in range(4):
            at = slice(q * quarter, (q + 1) * quarter)
            row = t * 4 + q
            out[t : t + 1, at] = (residual[t : t + 1, at] + total[row : row + 1]).astype(BF16)


def on_device(
    states,
    queries,
    new_keys,
    new_values,
    text_keys,
    text_values,
    text_length,
    image_keys,
    image_values,
    image_slot,
    block_list,
    block_count,
    image_first,
    image_count,
    out_weight,
    norm_gain,
    gate_weight,
    up_weight,
    down_weight,
):
    groups = lax.axis_size("group")
    depths = lax.axis_size("depth")
    ring = lax.axis_size("mp")
    requests, heads, width = queries.shape
    half = requests // depths
    features = states.shape[1]

    integers = (image_slot, block_list, block_count, image_first, image_count)
    in_place = [in_hbm(x) for x in (*integers, queries)]
    routed, plan = call(
        route_kernel,
        (
            jax.ShapeDtypeStruct((groups, 16, width), BF16),
            jax.ShapeDtypeStruct((2, requests * heads, 128), jnp.int32),
        ),
        [HBM] * 6,
        20_000_000_000,
        100_000,
        "route",
        scratch=[pltpu.SMEM(i.shape, jnp.int32) for i in integers]
        + [pltpu.VMEM(queries.shape, BF16), pltpu.SemaphoreType.DMA((len(in_place),))],
        out_specs=(VMEM, VMEM),
    )(*in_place)
    arrived = lax.all_to_all(routed, "group", 0, 0, tiled=True)
    arrived, queries = lax.optimization_barrier((arrived, queries))

    part = jax.ShapeDtypeStruct((half, 16, width), F32)
    own, other = call(
        text_kernel,
        (part, part),
        [HBM] + [VMEM] * 5,
        200_000_000,
        4_400_000,
        "text",
        scratch=[pltpu.SMEM(text_length.shape, jnp.int32), pltpu.SemaphoreType.DMA],
    )(in_hbm(text_length), queries, new_keys, new_values, text_keys, text_values)
    other = lax.ppermute(other, "depth", [(0, 1), (1, 0)])

    back = call(
        image_kernel,
        jax.ShapeDtypeStruct((groups, depths, 16, width), BF16),
        [VMEM] * 4,
        10_000_000_000,
        5_000_000,
        "image",
    )(own, arrived, image_keys, image_values)
    back, other = lax.optimization_barrier((back, other))
    back = lax.all_to_all(
        back.reshape(groups * depths, 16, width), ("group", "depth"), 0, 0, tiled=True
    )
    attention, mine, sent = call(
        merge_kernel,
        (
            jax.ShapeDtypeStruct((half, heads, width), BF16),
            jax.ShapeDtypeStruct((half, features), F32),
            jax.ShapeDtypeStruct((half, features), BF16),
        ),
        [VMEM] * 6,
        10_000_000_000,
        8_800_000,
        "merge",
        scratch=[
            pltpu.VMEM((half * heads, width), F32),
            pltpu.VMEM((half, heads, width), BF16),
            pltpu.SemaphoreType.DMA,
        ],
        out_specs=(HBM, VMEM, VMEM),
    )(plan, back, own, other, states, out_weight)
    passed = [
        lax.ppermute(sent, "mp", [(i, i ^ k) for i in range(ring)]) for k in (2, 3, 1)
    ]
    rest, normed = call(
        norm_kernel,
        (
            jax.ShapeDtypeStruct((2, features), F32),
            jax.ShapeDtypeStruct((groups, half, features), BF16),
        ),
        [VMEM] * 5,
        0,
        1_600_000,
        "norm",
    )(mine, *passed, norm_gain.reshape(1, features))
    tokens = lax.all_to_all(normed, "group", 0, 0, tiled=True).reshape(groups * half, features)
    peers = groups * ring
    down = call(
        feed_kernel,
        jax.ShapeDtypeStruct((peers, 8, features // 4), BF16),
        [VMEM] * 4,
        1_400_000_000,
        7_000_000,
        "feed",
        scratch=[pltpu.VMEM((features // 512, groups * half * 4, 128), F32)],
    )(tokens, gate_weight.T, up_weight.T, down_weight)
    gathered = lax.all_to_all(down, ("group", "mp"), 0, 0, tiled=True)
    layer_out = call(
        last_kernel,
        jax.ShapeDtypeStruct((2, features), BF16),
        [VMEM] * 2,
        0,
        1_300_000,
        "last",
    )(gathered, rest)
    return attention, layer_out


def solution(mesh):
    placed = (
        P(("group", "depth", "mp"), None),
        P("group", "mp", None),
        P("group", "mp", None),
        P("group", "mp", None),
        P("group", "mp", "depth", None),
        P("group", "mp", "depth", None),
        P("group"),
        P("group", "mp", None, None),
        P("group", "mp", None, None),
        P(),
        P(),
        P(),
        P("group"),
        P("group"),
        P("mp", None),
        P(),
        P(None, ("group", "mp")),
        P(None, ("group", "mp")),
        P(("group", "mp"), None),
    )
    return jax.shard_map(
        on_device,
        mesh=mesh,
        in_specs=placed,
        out_specs=(P(("group", "depth"), "mp", None), P(("group", "depth", "mp"), None)),
        check_vma=False,
    )
```
